256 devices in a mesh: facet: 8 (over x_hi, y), tm: 32 (over z, x_lo, core).
Axes of the slice: x: 4 (x_hi: 2, x_lo: 2; x = x_hi * 2 + x_lo), y: 4, z: 8, core: 2. Of those that a mesh axis runs over, the one named last changes fastest.
Arguments:
- visibilities: bfloat16 [2, 4096, 128], P(None, ('tm', 'facet')), may hold values from -6 to 6
- coordinates: bfloat16 [3, 4096, 128], P(None, ('tm', 'facet')), may hold values from -12 to 12
- station_screens: bfloat16 [2, 512, 2, 1024], P(None, 'tm'), may hold values from -5 to 5
- subgrid_stations: int32 [4096, 2], P('tm'), may hold values from 0 to 511, as said below
- subgrid_corners: int32 [4096, 2], P('tm'), may hold values from -32768 to 32736
- facet_member: int32 [4096, 8], P('tm', 'facet'), may hold values 0 or 1
Outputs:
- facets: float32 [2, 8, 512, 512], P(None, 'facet', 'tm')
The draws below stay inside these ranges and needn't reach their ends.
Inputs may be any that keep to these rules, and one draw needn't show every extreme that they name: `subgrid_stations`: the two stations of a subgrid differ.
All inputs are finite; a program needn't handle non-finite values. No bound on the sum of `facet_member` on one device may be relied on, other than what follows from the above.
Results may differ from the reference program's by a relative error of at most 0.013.
Values may be sent and summed in bfloat16 or wider, within the bound.
A program may use at most 64 MiB of HBM per device.

```python
import math
import jax
import jax.numpy as jnp
from jax import lax

STATIONS = 512
GRID = 65536
S = 32
NT = 128
SLABS = 2
FP = 512
NSUB = 4096
NFACETS = 8
N_TM = 32


def draw_subgrid_stations(key, part):
    first_key, second_key = jax.random.split(jax.random.fold_in(key, 17))
    first_station = jax.random.randint(first_key, (NSUB,), 0, STATIONS)
    step_size = jax.random.randint(second_key, (NSUB,), 1, STATIONS)
    second_station = (first_station + step_size) % STATIONS
    return jnp.stack([first_station, second_station], axis=1).astype(jnp.int32)


def place_ends(entries, rng, low, high):
    place = [jax.random.randint(jax.random.fold_in(rng, axis), (), 0, length) for axis, length in enumerate(entries.shape)]
    main_axis = entries.shape.index(max(entries.shape))
    beside = place[:main_axis] + [(place[main_axis] + 1) % entries.shape[main_axis]] + place[main_axis + 1:]
    return entries.at[tuple(place)].set(low).at[tuple(beside)].set(high)


def levels(key, extent, cuts, least, top_value):
    level, own = 1.0, jax.random.fold_in(key, 6)
    for axis_at, shards_of in cuts:
        heights = jnp.exp(jax.random.uniform(jax.random.fold_in(own, axis_at), (shards_of,), jnp.float32, least / len(cuts), top_value / len(cuts)))
        level = level * jnp.repeat(heights, extent[axis_at] // shards_of).reshape([-1 if axis == axis_at else 1 for axis in range(len(extent))])
    return level


def scatter_about(stream_key, extent, scale, bound, shards=(), kind=jnp.bfloat16):
    level = levels(stream_key, extent, shards, -0.22, 0.18) if shards else 1.0
    entries = jax.random.normal(stream_key, extent, jnp.float32) * scale * level
    return jnp.minimum(jnp.maximum(entries, -bound), bound).astype(kind)


def setup_inputs(seed: int = 0) -> dict:
    streams_of = jax.random.split(jax.random.key(seed), 7)
    return {
        "visibilities": scatter_about(streams_of[0], (2, NSUB, NT), 1.0, 6.0, ((1, 256),)),
        "coordinates": jnp.clip(jax.random.uniform(streams_of[1], (3, NSUB, NT), jnp.float32, -12.0, 12.0) * levels(streams_of[1], (3, NSUB, NT), ((1, 256),), -0.4, 0.0), -12.0, 12.0).astype(jnp.bfloat16),
        "station_screens": scatter_about(streams_of[2], (SLABS, STATIONS, 2, S * S), 0.7, 5.0, ((1, 32),)),
        "subgrid_stations": draw_subgrid_stations(jax.random.fold_in(streams_of[6], 71), 0),
        "subgrid_corners": place_ends(jax.random.randint(streams_of[4], (NSUB, 2), 0 - GRID // 2, GRID // 2 - S + 1), jax.random.fold_in(streams_of[4], 1), 0 - GRID // 2, (GRID // 2 - S + 1) - 1).astype(jnp.int32),
        "facet_member": place_ends((jax.random.randint(streams_of[5], (NSUB, NFACETS), 0, 4) < 3).astype(jnp.int32), jax.random.fold_in(streams_of[5], 1), 0, 1),
    }


two_pi = 2.0 * math.pi

def wrap_product(first_factor, second_factor):
    high_part = first_factor // 256
    low_part = first_factor % 256
    return (high_part * second_factor % GRID * 256 + low_part * second_factor) % GRID

def batched(form, first_factor, second_factor):
    return jnp.einsum(form, first_factor.astype(jnp.float32), second_factor.astype(jnp.float32))

def taper_flat():
    centre = jnp.sin(math.pi * (jnp.arange(S, dtype=jnp.float32) + 0.5) / S)
    return (centre[:, None] * centre[None, :]).reshape(S * S)

def dft_table():
    offsets = jnp.arange(S, dtype=jnp.int32) - S // 2
    phases = (offsets[:, None] * offsets[None, :] % S).astype(jnp.float32)
    angles = -two_pi * phases / S
    factor = 1.0 / math.sqrt(S)
    return ((jnp.cos(angles) * factor).astype(jnp.bfloat16), (jnp.sin(angles) * factor).astype(jnp.bfloat16))

def grid_subgrids(visibility_block, coordinate_block, first_screens, second_screens):
    cell_coords = (jnp.arange(S, dtype=jnp.float32) - S // 2) / S
    squares = cell_coords * cell_coords
    vis_real = visibility_block[0].astype(jnp.float32)[:, None, :]
    vis_imag = visibility_block[1].astype(jnp.float32)[:, None, :]
    shift_u = coordinate_block[0].astype(jnp.float32)[:, None, :]
    shift_v = coordinate_block[1].astype(jnp.float32)[:, None, :]
    shift_w = coordinate_block[2].astype(jnp.float32)[:, None, :]
    angle_left = two_pi * shift_u * cell_coords[None, :, None] - math.pi * shift_w * squares[None, :, None]
    angle_right = two_pi * shift_v * cell_coords[None, :, None] - math.pi * shift_w * squares[None, :, None]
    cos_left = jnp.cos(angle_left)
    sin_left = jnp.sin(angle_left)
    left_real = (vis_real * cos_left - vis_imag * sin_left).astype(jnp.bfloat16)
    left_imag = (vis_real * sin_left + vis_imag * cos_left).astype(jnp.bfloat16)
    right_real = jnp.cos(angle_right).astype(jnp.bfloat16)
    right_imag = jnp.sin(angle_right).astype(jnp.bfloat16)
    image_real = batched('sit,sjt->sij', left_real, right_real) - batched('sit,sjt->sij', left_imag, right_imag)
    image_imag = batched('sit,sjt->sij', left_real, right_imag) + batched('sit,sjt->sij', left_imag, right_real)
    row_count = image_real.shape[0]
    image_real = image_real.reshape(row_count, S * S)
    image_imag = image_imag.reshape(row_count, S * S)
    taper = taper_flat()
    first_real = first_screens[:, 0].astype(jnp.float32)
    first_imag = first_screens[:, 1].astype(jnp.float32)
    second_real = second_screens[:, 0].astype(jnp.float32)
    second_imag = second_screens[:, 1].astype(jnp.float32)
    weight_real = taper * (first_real * second_real + first_imag * second_imag)
    weight_imag = taper * (first_real * second_imag - first_imag * second_real)
    weighted_real = (weight_real * image_real - weight_imag * image_imag).astype(jnp.bfloat16).reshape(row_count, S, S)
    weighted_imag = (weight_real * image_imag + weight_imag * image_real).astype(jnp.bfloat16).reshape(row_count, S, S)
    table_real, table_imag = dft_table()
    half_real = (batched('ai,sij->saj', table_real, weighted_real) - batched('ai,sij->saj', table_imag, weighted_imag)).astype(jnp.bfloat16)
    half_imag = (batched('ai,sij->saj', table_real, weighted_imag) + batched('ai,sij->saj', table_imag, weighted_real)).astype(jnp.bfloat16)
    grid_real = (batched('saj,bj->sab', half_real, table_real) - batched('saj,bj->sab', half_imag, table_imag)).astype(jnp.bfloat16)
    grid_imag = (batched('saj,bj->sab', half_real, table_imag) + batched('saj,bj->sab', half_imag, table_real)).astype(jnp.bfloat16)
    return jnp.stack([grid_real, grid_imag], axis=1)

def facet_anchor(facet_number):
    stride_quarter = GRID // FP // 4
    return (facet_number % 4 * stride_quarter, facet_number // 4 % 4 * stride_quarter)

def pixel_numbers(anchor, first_row, row_count):
    stride = GRID // FP
    return (anchor + (first_row + jnp.arange(row_count, dtype=jnp.int32)) * stride) % GRID

def edge_table(pixels):
    columns = jnp.arange(S, dtype=jnp.int32)
    phases = (pixels[:, None] * columns[None, :] % GRID).astype(jnp.float32)
    angles = two_pi * phases / GRID
    factor = 1.0 / math.sqrt(S)
    return ((jnp.cos(angles) * factor).astype(jnp.bfloat16), (jnp.sin(angles) * factor).astype(jnp.bfloat16))

def shift_table(corner, pixels):
    phases = wrap_product((corner % GRID)[:, None], pixels[None, :]).astype(jnp.float32)
    angles = two_pi * phases / GRID
    return (jnp.cos(angles), jnp.sin(angles))

def block_term(grid_block, corner_block, member_block, pixels_x, pixels_y, tables):
    edge_real_x, edge_imag_x, edge_real_y, edge_imag_y = tables
    grid_real = grid_block[:, 0]
    grid_imag = grid_block[:, 1]
    mixed_real = batched('xa,sab->sxb', edge_real_x, grid_real) - batched('xa,sab->sxb', edge_imag_x, grid_imag)
    mixed_imag = batched('xa,sab->sxb', edge_real_x, grid_imag) + batched('xa,sab->sxb', edge_imag_x, grid_real)
    shift_real_x, shift_imag_x = shift_table(corner_block[:, 0], pixels_x)
    weight = member_block.astype(jnp.float32)[:, None, None]
    left_real = (weight * (shift_real_x[:, :, None] * mixed_real - shift_imag_x[:, :, None] * mixed_imag)).astype(jnp.bfloat16)
    left_imag = (weight * (shift_real_x[:, :, None] * mixed_imag + shift_imag_x[:, :, None] * mixed_real)).astype(jnp.bfloat16)
    shift_real_y, shift_imag_y = shift_table(corner_block[:, 1], pixels_y)
    edge_y_real = edge_real_y.astype(jnp.float32)[None]
    edge_y_imag = edge_imag_y.astype(jnp.float32)[None]
    right_real = (shift_real_y[:, :, None] * edge_y_real - shift_imag_y[:, :, None] * edge_y_imag).astype(jnp.bfloat16)
    right_imag = (shift_real_y[:, :, None] * edge_y_imag + shift_imag_y[:, :, None] * edge_y_real).astype(jnp.bfloat16)
    out_real = batched('sxb,syb->xy', left_real, right_real) - batched('sxb,syb->xy', left_imag, right_imag)
    out_imag = batched('sxb,syb->xy', left_real, right_imag) + batched('sxb,syb->xy', left_imag, right_real)
    return (out_real, out_imag)

def reference(visibilities, coordinates, station_screens, subgrid_stations, subgrid_corners, facet_member):
    total_count = visibilities.shape[1]
    slab_index = jnp.arange(total_count, dtype=jnp.int32) // (total_count // SLABS)
    first_screens = station_screens[slab_index, subgrid_stations[:, 0]]
    second_screens = station_screens[slab_index, subgrid_stations[:, 1]]
    subgrid_tiles = grid_subgrids(visibilities, coordinates, first_screens, second_screens)
    block_size = total_count // N_TM
    grid_blocks = subgrid_tiles.reshape(N_TM, block_size, 2, S, S)
    corner_blocks = subgrid_corners.reshape(N_TM, block_size, 2)
    facet_total = facet_member.shape[1]
    member_blocks = jnp.transpose(facet_member).reshape(facet_total, N_TM, block_size)
    scale_factor = 1.0 / math.sqrt(visibilities.shape[2] * total_count)

    def one_facet(facet_item):
        facet_number, members = facet_item
        anchor_x, anchor_y = facet_anchor(facet_number)
        pixels_x = pixel_numbers(anchor_x, 0, FP)
        pixels_y = pixel_numbers(anchor_y, 0, FP)
        tables = edge_table(pixels_x) + edge_table(pixels_y)
        zeros_start = jnp.zeros((FP, FP), jnp.float32)

        def add_block(running, block_item):
            part_real, part_imag = block_term(block_item[0], block_item[1], block_item[2], pixels_x, pixels_y, tables)
            return ((running[0] + part_real, running[1] + part_imag), None)
        totals, unused = lax.scan(add_block, (zeros_start, zeros_start), (grid_blocks, corner_blocks, members))
        return jnp.stack([totals[0], totals[1]]) * scale_factor
    numbers = jnp.arange(facet_total, dtype=jnp.int32)
    result = lax.map(one_facet, (numbers, member_blocks))
    return jnp.transpose(result, (1, 0, 2, 3))
```

```python
import functools
import math

import jax
import jax.numpy as jnp
import numpy as np
from jax import lax
from jax.experimental import pallas as pl
from jax.experimental.pallas import tpu as pltpu
from jax.sharding import PartitionSpec as P

GRID = 65536
S = 32
NT = 128
SLABS = 2
FP = 512
LANES = 128
GROUPS = 8
RADIX = 4
MESH = pl.DeviceIdType.MESH
F32 = jnp.float32
BF16 = jnp.bfloat16


def rounded(values):
    return np.asarray(values, np.float32).astype(jnp.bfloat16)


def complex_block(values):
    return np.block([[values.real, values.imag], [-values.imag, values.real]])


def dft_rows_table():
    offsets = np.arange(S) - S // 2
    table = np.exp(-2j * np.pi * (np.outer(offsets, offsets) % S) / S) / math.sqrt(S)
    return rounded(complex_block(np.kron(np.eye(RADIX), table.T)))


def dft_columns_table():
    tables = []
    for a_lo in range(GROUPS):
        offset = 8 * (np.arange(RADIX) - 2) + a_lo
        factor = (-1.0) ** a_lo * np.exp(-2j * np.pi * np.outer(np.arange(RADIX), offset) / S) / math.sqrt(S)
        tables.append(rounded(complex_block(np.kron(factor, np.eye(S)))))
    return np.stack(tables)


def facet_table():
    angles = 2.0 * np.pi * (np.outer(np.arange(FP), np.arange(FP)) % FP) / FP
    return rounded(np.concatenate([np.cos(angles), np.sin(angles)], axis=1))


def taper_table():
    centre = np.sin(np.pi * (np.arange(S) + 0.5) / S)
    return np.outer(centre, centre).reshape(GROUPS, LANES).astype(np.float32)


def cos_sin(turns):
    rest = turns - jnp.round(turns)
    angle = rest * math.pi
    square = angle * angle
    sin_half = -1.0 / 39916800.0
    for term in (1.0 / 362880.0, -1.0 / 5040.0, 1.0 / 120.0, -1.0 / 6.0, 1.0):
        sin_half = sin_half * square + term
    sin_half = sin_half * angle
    cos_half = 1.0 / 479001600.0
    for term in (-1.0 / 3628800.0, 1.0 / 40320.0, -1.0 / 720.0, 1.0 / 24.0, -0.5, 1.0):
        cos_half = cos_half * square + term
    return 1.0 - 2.0 * sin_half * sin_half, 2.0 * sin_half * cos_half


def dot(left, right):
    return jnp.dot(left, right, preferred_element_type=F32)


def own_images(inputs_ref, image_ref):
    row = lax.broadcasted_iota(jnp.int32, (S, NT), 0)
    cell_left = (RADIX * (row % GROUPS) + row // GROUPS - S // 2).astype(F32) / S
    cell_right = (row - S // 2).astype(F32) / S
    half_left = cell_left * cell_left * 0.5
    half_right = cell_right * cell_right * 0.5
    lane_block = lax.broadcasted_iota(jnp.int32, (GROUPS, LANES), 1) // S

    def one(number, carry):
        vis_real, vis_imag, shift_u, shift_v, shift_w = (
            inputs_ref[part, pl.ds(number, 1), :] for part in range(5)
        )
        cos_left, sin_left = cos_sin(shift_u * cell_left - shift_w * half_left)
        cos_right, sin_right = cos_sin(shift_v * cell_right - shift_w * half_right)
        left = jnp.concatenate(
            [vis_real * cos_left - vis_imag * sin_left, vis_real * sin_left + vis_imag * cos_left], axis=0
        ).astype(BF16)
        right = jnp.concatenate([cos_right] * RADIX + [sin_right] * RADIX, axis=0).astype(BF16)
        product = lax.dot_general(left, right, (((1,), (1,)), ((), ())), preferred_element_type=F32)
        real = product[:S, :LANES] - product[S:, LANES:]
        imag = product[:S, LANES:] + product[S:, :LANES]
        for part, whole in ((0, real), (1, imag)):
            chosen = whole[:GROUPS]
            for block in range(1, RADIX):
                chosen = jnp.where(lane_block == block, whole[GROUPS * block : GROUPS * (block + 1)], chosen)
            for block in range(GROUPS):
                image_ref[block, part, pl.ds(number, 1), :] = chosen[block : block + 1]
        return carry

    lax.fori_loop(0, inputs_ref.shape[1], one, 0)


def rows_kernel(
    facets,
    times,
    vis_ref,
    coord_ref,
    screen_ref,
    station_ref,
    taper_ref,
    table_ref,
    out_ref,
    inputs,
    image,
    images,
    screens,
    mixed,
    image_send,
    image_recv,
    screen_send,
    screen_recv,
    out_send,
    out_recv,
):
    facet = lax.axis_index("facet")
    time = lax.axis_index("tm")
    barrier = pltpu.get_barrier_semaphore()
    for step in range(1, facets):
        pl.semaphore_signal(
            barrier, inc=1, device_id={"facet": lax.rem(facet + step, facets)}, device_id_type=MESH
        )
    for step in range(1, times):
        pl.semaphore_signal(barrier, inc=1, device_id={"tm": lax.rem(time + step, times)}, device_id_type=MESH)

    inputs[0:2] = vis_ref[...].astype(F32)
    inputs[2:5] = coord_ref[...].astype(F32)
    pl.semaphore_wait(barrier, facets - 1 + times - 1)

    screen_copies = []
    for step in range(1, times):
        target = lax.rem(time + step, times)
        copy = pltpu.make_async_remote_copy(
            src_ref=screen_ref.at[target // (times // SLABS)],
            dst_ref=screens.at[time],
            send_sem=screen_send.at[step],
            recv_sem=screen_recv.at[step],
            device_id={"tm": target},
            device_id_type=MESH,
        )
        copy.start()
        screen_copies.append(copy)
    screens[time] = screen_ref[time // (times // SLABS)]

    own_images(inputs, image)

    image_copies = []
    for step in range(1, facets):
        target = lax.rem(facet + step, facets)
        copy = pltpu.make_async_remote_copy(
            src_ref=image.at[target],
            dst_ref=images.at[facet],
            send_sem=image_send.at[step],
            recv_sem=image_recv.at[step],
            device_id={"facet": target},
            device_id_type=MESH,
        )
        copy.start()
        image_copies.append(copy)
    images[facet] = image[facet]
    for copy in image_copies + screen_copies:
        copy.wait()

    count = station_ref.shape[0]
    stations = screens.shape[0] * screens.shape[2]
    screen_pair = jnp.concatenate(
        [screens[:, 0].reshape(stations, LANES), screens[:, 1].reshape(stations, LANES)], axis=1
    )
    station = lax.broadcasted_iota(jnp.int32, (count, stations), 1)
    first = dot((station == station_ref[:, 0:1]).astype(F32).astype(BF16), screen_pair)
    second = dot((station == station_ref[:, 1:2]).astype(F32).astype(BF16), screen_pair)
    first_real, first_imag = first[:, :LANES], first[:, LANES:]
    second_real, second_imag = second[:, :LANES], second[:, LANES:]
    taper = taper_ref[pl.ds(facet, 1), :]
    weight_real = taper * (first_real * second_real + first_imag * second_imag)
    weight_imag = taper * (first_real * second_imag - first_imag * second_real)
    image_real = images[:, 0].reshape(count, LANES)
    image_imag = images[:, 1].reshape(count, LANES)
    weighted = jnp.concatenate(
        [
            weight_real * image_real - weight_imag * image_imag,
            weight_real * image_imag + weight_imag * image_real,
        ],
        axis=1,
    ).astype(BF16)
    mixed[...] = dot(weighted, table_ref[...]).astype(BF16)

    out_copies = []
    for step in range(1, facets):
        copy = pltpu.make_async_remote_copy(
            src_ref=mixed,
            dst_ref=out_ref.at[facet],
            send_sem=out_send.at[step],
            recv_sem=out_recv.at[step],
            device_id={"facet": lax.rem(facet + step, facets)},
            device_id_type=MESH,
        )
        copy.start()
        out_copies.append(copy)
    out_ref[facet] = mixed[...]
    for copy in out_copies:
        copy.wait()


def gather_rows(visibilities, coordinates, screens, stations, facets, times):
    own = visibilities.shape[1]
    count = stations.shape[0]
    vmem = pl.BlockSpec(memory_space=pltpu.VMEM)
    return pl.pallas_call(
        functools.partial(rows_kernel, facets, times),
        out_shape=jax.ShapeDtypeStruct((facets, count, 2 * LANES), BF16),
        in_specs=[vmem] * 6,
        out_specs=vmem,
        scratch_shapes=[
            pltpu.VMEM((5, own, NT), F32),
            pltpu.VMEM((GROUPS, 2, own, LANES), F32),
            pltpu.VMEM((GROUPS, 2, own, LANES), F32),
            pltpu.VMEM((times,) + screens.shape[1:], BF16),
            pltpu.VMEM((count, 2 * LANES), BF16),
            pltpu.SemaphoreType.DMA((facets,)),
            pltpu.SemaphoreType.DMA((facets,)),
            pltpu.SemaphoreType.DMA((times,)),
            pltpu.SemaphoreType.DMA((times,)),
            pltpu.SemaphoreType.DMA((facets,)),
            pltpu.SemaphoreType.DMA((facets,)),
        ],
        compiler_params=pltpu.CompilerParams(collective_id=0, has_side_effects=True),
        name="subgrid_rows",
    )(
        visibilities,
        coordinates,
        screens,
        stations,
        jnp.asarray(taper_table()),
        jnp.asarray(dft_rows_table()),
    )


def eight_point(parts):
    root = math.sqrt(0.5)

    def add(a, b):
        return a[0] + b[0], a[1] + b[1]

    def sub(a, b):
        return a[0] - b[0], a[1] - b[1]

    def minus_i(a):
        return a[1], -a[0]

    def four_point(p):
        even_sum, even_diff = add(p[0], p[2]), sub(p[0], p[2])
        odd_sum, odd_diff = add(p[1], p[3]), minus_i(sub(p[1], p[3]))
        return add(even_sum, odd_sum), add(even_diff, odd_diff), sub(even_sum, odd_sum), sub(even_diff, odd_diff)

    even = four_point(parts[0::2])
    odd = list(four_point(parts[1::2]))
    odd[1] = ((odd[1][0] + odd[1][1]) * root, (odd[1][1] - odd[1][0]) * root)
    odd[2] = minus_i(odd[2])
    odd[3] = ((odd[3][1] - odd[3][0]) * root, -(odd[3][0] + odd[3][1]) * root)
    return [add(even[k], odd[k]) for k in range(4)] + [sub(even[k], odd[k]) for k in range(4)]


def fold_kernel(
    facet_ref,
    corner_smem,
    corner_ref,
    member_ref,
    mixed_ref,
    columns_ref,
    edge_ref,
    out_ref,
    spread,
    cells,
    folded,
    lines,
):
    count = corner_ref.shape[0]
    anchor_x = facet_ref[0] % 4 * (GRID // FP // 4)
    anchor_y = facet_ref[0] // 4 % 4 * (GRID // FP // 4)
    folded[...] = jnp.zeros_like(folded)

    rows = 16

    def eight(step, carry):
        at = pl.ds(pl.multiple_of(step * rows, rows), rows)
        parts = []
        for source in range(GROUPS):
            pair = mixed_ref[source, at, :].astype(F32)
            parts.append((pair[:, :LANES], pair[:, LANES:]))
        for a_lo, value in enumerate(eight_point(parts)):
            spread[a_lo, at, :] = jnp.concatenate(value, axis=1).astype(BF16)
        return carry

    lax.fori_loop(0, count // rows, eight, 0)

    phase = (
        (corner_ref[:, 0:1] & (GRID - 1)) * anchor_x + (corner_ref[:, 1:2] & (GRID - 1)) * anchor_y
    ) & (GRID - 1)
    cos_corner, sin_corner = cos_sin(phase.astype(F32) * (1.0 / GRID))
    member = member_ref[...].astype(F32)
    cos_corner = cos_corner * member
    sin_corner = sin_corner * member
    lane = lax.broadcasted_iota(jnp.int32, (1, LANES), 1)
    for a_lo in range(GROUPS):
        offset = (8 * (lane // S) + a_lo) * anchor_x + lane % S * anchor_y
        cos_cell, sin_cell = cos_sin(offset.astype(F32) * (1.0 / GRID))
        cos_all = cos_corner * cos_cell - sin_corner * sin_cell
        sin_all = cos_corner * sin_cell + sin_corner * cos_cell
        value = dot(spread[a_lo], columns_ref[a_lo])
        real, imag = value[:, :LANES], value[:, LANES:]
        cells[pl.ds(a_lo * count, count), :] = real * cos_all - imag * sin_all
        cells[pl.ds((GROUPS + a_lo) * count, count), :] = real * sin_all + imag * cos_all

    lane8 = lax.broadcasted_iota(jnp.int32, (8, LANES), 1)

    def place(number, carry):
        first_u = corner_smem[number, 0] & (FP - 1)
        first_v = corner_smem[number, 1] & (FP - 1)
        tile = first_v // LANES
        within = first_v % LANES
        here = (lane8 >= within) & (lane8 < within + S)
        there = lane8 < within + S - LANES
        for part in range(2):
            block = cells[pl.ds(part * GROUPS * count + number, GROUPS, stride=count), :]
            for a_hi in range(RADIX):
                moved = pltpu.roll(block, (within - S * a_hi) & (LANES - 1), 1)
                at = pl.ds(first_u + 8 * a_hi, 8)
                folded[part, tile, at, :] += jnp.where(here, moved, 0.0)
                folded[part, tile + 1, at, :] += jnp.where(there, moved, 0.0)
        return carry

    lax.fori_loop(0, count, place, 0)

    for part in range(2):
        folded[part, :, 0:S, :] += folded[part, :, FP : FP + S, :]
        folded[part, 0] += folded[part, FP // LANES]
    tiles = FP // LANES
    for tile in range(tiles):
        real, imag = folded[0, tile, 0:FP, :], folded[1, tile, 0:FP, :]
        lines[0:FP, pl.ds(tile * LANES, LANES)] = real.astype(BF16)
        lines[FP : 2 * FP, pl.ds(tile * LANES, LANES)] = (-imag).astype(BF16)
        lines[0:FP, pl.ds(FP + tile * LANES, LANES)] = imag.astype(BF16)
        lines[FP : 2 * FP, pl.ds(FP + tile * LANES, LANES)] = real.astype(BF16)
    width = 256

    def transform(step, carry):
        at = pl.ds(pl.multiple_of(step * width, width), width)
        out_ref[:, at] = dot(edge_ref[...], lines[:, at]).astype(BF16)
        return carry

    lax.fori_loop(0, 2 * FP // width, transform, 0)


def fold_facet(facet, corners, members, mixed, edges):
    count = corners.shape[0]
    vmem = pl.BlockSpec(memory_space=pltpu.VMEM)
    smem = pl.BlockSpec(memory_space=pltpu.SMEM)
    return pl.pallas_call(
        fold_kernel,
        out_shape=jax.ShapeDtypeStruct((FP, 2 * FP), BF16),
        in_specs=[smem, smem, vmem, vmem, vmem, vmem, vmem],
        out_specs=vmem,
        scratch_shapes=[
            pltpu.VMEM((GROUPS, count, 2 * LANES), BF16),
            pltpu.VMEM((2 * GROUPS * count, LANES), F32),
            pltpu.VMEM((2, FP // LANES + 1, FP + S, LANES), F32),
            pltpu.VMEM((2 * FP, 2 * FP), BF16),
        ],
        name="fold_facet",
    )(facet.reshape(1), corners, corners, members, mixed, jnp.asarray(dft_columns_table()), edges)


def sum_kernel(scale, times, lines_ref, edge_ref, out_ref, pair, half, whole, send, recv, pair_send, pair_recv):
    time = lax.axis_index("tm")
    chips = times // 2
    core = lax.rem(time, 2)
    chip = time // 2
    other = time + 1 - 2 * core
    barrier = pltpu.get_barrier_semaphore()
    pl.semaphore_signal(barrier, inc=1, device_id={"tm": other}, device_id_type=MESH)
    for step in range(1, chips):
        target = lax.rem(chip + step, chips) * 2 + core
        pl.semaphore_signal(barrier, inc=1, device_id={"tm": target}, device_id_type=MESH)
    pl.semaphore_wait(barrier, chips)

    exchange = pltpu.make_async_remote_copy(
        src_ref=lines_ref.at[:, 1 - core],
        dst_ref=pair,
        send_sem=pair_send,
        recv_sem=pair_recv,
        device_id={"tm": other},
        device_id_type=MESH,
    )
    exchange.start()
    exchange.wait()
    half[...] = (lines_ref[:, core].astype(F32) + pair[...].astype(F32)).astype(BF16)
    copies = []
    for step in range(1, chips):
        target = lax.rem(chip + step, chips)
        copy = pltpu.make_async_remote_copy(
            src_ref=half.at[target],
            dst_ref=whole.at[chip],
            send_sem=send.at[step],
            recv_sem=recv.at[step],
            device_id={"tm": target * 2 + core},
            device_id_type=MESH,
        )
        copy.start()
        copies.append(copy)
    whole[chip] = half[chip]
    for copy in copies:
        copy.wait()
    total = whole[0].astype(F32)
    for source in range(1, chips):
        total = total + whole[source].astype(F32)
    total = total.astype(BF16)
    real, imag = total[:, :FP], total[:, FP:]
    cos_part, sin_part = edge_ref[:, :FP], edge_ref[:, FP:]
    out_ref[0] = (dot(real, cos_part) - dot(imag, sin_part)) * scale
    out_ref[1] = (dot(real, sin_part) + dot(imag, cos_part)) * scale


def sum_facet(lines, edges, scale, times):
    chips = times // 2
    rows = FP // times
    vmem = pl.BlockSpec(memory_space=pltpu.VMEM)
    return pl.pallas_call(
        functools.partial(sum_kernel, scale, times),
        out_shape=jax.ShapeDtypeStruct((2, rows, FP), F32),
        in_specs=[vmem] * 2,
        out_specs=vmem,
        scratch_shapes=[
            pltpu.VMEM((chips, rows, 2 * FP), BF16),
            pltpu.VMEM((chips, rows, 2 * FP), BF16),
            pltpu.VMEM((chips, rows, 2 * FP), BF16),
            pltpu.SemaphoreType.DMA((chips,)),
            pltpu.SemaphoreType.DMA((chips,)),
            pltpu.SemaphoreType.DMA,
            pltpu.SemaphoreType.DMA,
        ],
        compiler_params=pltpu.CompilerParams(collective_id=1, has_side_effects=True),
        name="sum_facet",
    )(lines.reshape(chips, 2, rows, 2 * FP), edges)


def per_device(
    visibilities, coordinates, station_screens, subgrid_stations, subgrid_corners, facet_member
):
    times = lax.axis_size("tm")
    facets = lax.axis_size("facet")
    facet = lax.axis_index("facet")
    screens = jnp.transpose(
        lax.dynamic_slice_in_dim(station_screens, facet * LANES, LANES, axis=3), (0, 2, 1, 3)
    )
    mixed = gather_rows(visibilities, coordinates, screens, subgrid_stations, facets, times)
    edges = jnp.asarray(facet_table())
    lines = fold_facet(facet, subgrid_corners, facet_member, mixed, edges)
    total_count = visibilities.shape[1] * facets * times
    scale = 1.0 / (S * math.sqrt(visibilities.shape[2] * total_count))
    own_rows = sum_facet(lines, edges, scale, times)
    return own_rows[:, None]


def solution(mesh):
    in_specs = (
        P(None, ("tm", "facet"), None),
        P(None, ("tm", "facet"), None),
        P(None, "tm", None, None),
        P("tm", None),
        P("tm", None),
        P("tm", "facet"),
    )
    out_specs = P(None, "facet", "tm", None)
    return jax.shard_map(
        per_device, mesh=mesh, in_specs=in_specs, out_specs=out_specs, check_vma=False
    )
```

```python
import functools
import math

import jax
import jax.numpy as jnp
import numpy as np
from jax import lax
from jax.experimental import pallas as pl
from jax.experimental.pallas import tpu as pltpu
from jax.sharding import PartitionSpec as P

UNROLL = 16
GRID = 65536
S = 32
NT = 128
SLABS = 2
FP = 512
LANES = 128
GROUPS = 8
RADIX = 4
MESH = pl.DeviceIdType.MESH
F32 = jnp.float32
BF16 = jnp.bfloat16


def rounded(values):
    return np.asarray(values, np.float32).astype(jnp.bfloat16)


def complex_block(values):
    return np.block([[values.real, values.imag], [-values.imag, values.real]])


def dft_rows_table():
    offsets = np.arange(S) - S // 2
    table = np.exp(-2j * np.pi * (np.outer(offsets, offsets) % S) / S) / math.sqrt(S)
    return rounded(complex_block(np.kron(np.eye(RADIX), table.T)))


def dft_columns_table():
    tables = []
    for a_lo in range(GROUPS):
        offset = 8 * (np.arange(RADIX) - 2) + a_lo
        factor = (-1.0) ** a_lo * np.exp(-2j * np.pi * np.outer(np.arange(RADIX), offset) / S) / math.sqrt(S)
        tables.append(rounded(complex_block(np.kron(factor, np.eye(S)))))
    return np.stack(tables)


def facet_table():
    angles = 2.0 * np.pi * (np.outer(np.arange(FP), np.arange(FP)) % FP) / FP
    return rounded(np.concatenate([np.cos(angles), np.sin(angles)], axis=1))


def facet_rows_table():
    tables = []
    for residue in range(4):
        angles = 2.0 * np.pi * (np.outer(np.arange(FP // 4), np.arange(residue, FP, 4)) % FP) / FP
        tables.append(rounded(complex_block(np.exp(-1j * angles))))
    return np.stack(tables)


def taper_table():
    centre = np.sin(np.pi * (np.arange(S) + 0.5) / S)
    return np.outer(centre, centre).reshape(GROUPS, LANES).astype(np.float32)


def cos_sin(turns):
    rest = turns - jnp.round(turns)
    angle = rest * math.pi
    square = angle * angle
    sin_half = -1.0 / 39916800.0
    for term in (1.0 / 362880.0, -1.0 / 5040.0, 1.0 / 120.0, -1.0 / 6.0, 1.0):
        sin_half = sin_half * square + term
    sin_half = sin_half * angle
    cos_half = 1.0 / 479001600.0
    for term in (-1.0 / 3628800.0, 1.0 / 40320.0, -1.0 / 720.0, 1.0 / 24.0, -0.5, 1.0):
        cos_half = cos_half * square + term
    return 1.0 - 2.0 * sin_half * sin_half, 2.0 * sin_half * cos_half


def dot(left, right):
    return jnp.dot(left, right, preferred_element_type=F32)


def own_images(inputs_ref, image_ref):
    row = lax.broadcasted_iota(jnp.int32, (S, NT), 0)
    cell_left = (RADIX * (row % GROUPS) + row // GROUPS - S // 2).astype(F32) / S
    cell_right = (row - S // 2).astype(F32) / S
    half_left = cell_left * cell_left * 0.5
    half_right = cell_right * cell_right * 0.5
    lane_block = lax.broadcasted_iota(jnp.int32, (GROUPS, LANES), 1) // S

    def one(number, carry):
        vis_real, vis_imag, shift_u, shift_v, shift_w = (
            inputs_ref[part, pl.ds(number, 1), :] for part in range(5)
        )
        cos_left, sin_left = cos_sin(shift_u * cell_left - shift_w * half_left)
        cos_right, sin_right = cos_sin(shift_v * cell_right - shift_w * half_right)
        left = jnp.concatenate(
            [vis_real * cos_left - vis_imag * sin_left, vis_real * sin_left + vis_imag * cos_left], axis=0
        ).astype(BF16)
        right = jnp.concatenate([cos_right] * RADIX + [sin_right] * RADIX, axis=0).astype(BF16)
        product = lax.dot_general(left, right, (((1,), (1,)), ((), ())), preferred_element_type=F32)
        real = product[:S, :LANES] - product[S:, LANES:]
        imag = product[:S, LANES:] + product[S:, :LANES]
        for part, whole in ((0, real), (1, imag)):
            chosen = whole[:GROUPS]
            for block in range(1, RADIX):
                chosen = jnp.where(lane_block == block, whole[GROUPS * block : GROUPS * (block + 1)], chosen)
            for block in range(GROUPS):
                image_ref[block, part, pl.ds(number, 1), :] = chosen[block : block + 1]
        return carry

    lax.fori_loop(0, inputs_ref.shape[1], one, 0)


def rows_kernel(
    facets,
    times,
    vis_ref,
    coord_ref,
    screen_ref,
    station_ref,
    taper_ref,
    table_ref,
    out_ref,
    inputs,
    image,
    images,
    screens,
    mixed,
    image_send,
    image_recv,
    screen_send,
    screen_recv,
    out_send,
    out_recv,
):
    facet = lax.axis_index("facet")
    time = lax.axis_index("tm")
    barrier = pltpu.get_barrier_semaphore()
    for step in range(1, facets):
        pl.semaphore_signal(
            barrier, inc=1, device_id={"facet": lax.rem(facet + step, facets)}, device_id_type=MESH
        )
    for step in range(1, times):
        pl.semaphore_signal(barrier, inc=1, device_id={"tm": lax.rem(time + step, times)}, device_id_type=MESH)

    inputs[0:2] = vis_ref[...].astype(F32)
    inputs[2:5] = coord_ref[...].astype(F32)
    pl.semaphore_wait(barrier, facets - 1 + times - 1)

    screen_copies = []
    for step in range(1, times):
        target = lax.rem(time + step, times)
        copy = pltpu.make_async_remote_copy(
            src_ref=screen_ref.at[target // (times // SLABS)],
            dst_ref=screens.at[time],
            send_sem=screen_send.at[step],
            recv_sem=screen_recv.at[step],
            device_id={"tm": target},
            device_id_type=MESH,
        )
        copy.start()
        screen_copies.append(copy)
    screens[time] = screen_ref[time // (times // SLABS)]

    own_images(inputs, image)

    image_copies = []
    for step in range(1, facets):
        target = lax.rem(facet + step, facets)
        copy = pltpu.make_async_remote_copy(
            src_ref=image.at[target],
            dst_ref=images.at[facet],
            send_sem=image_send.at[step],
            recv_sem=image_recv.at[step],
            device_id={"facet": target},
            device_id_type=MESH,
        )
        copy.start()
        image_copies.append(copy)
    images[facet] = image[facet]
    for copy in image_copies + screen_copies:
        copy.wait()

    count = station_ref.shape[1]
    stations = screens.shape[0] * screens.shape[2]
    screen_pair = jnp.concatenate(
        [screens[:, 0].reshape(stations, LANES), screens[:, 1].reshape(stations, LANES)], axis=1
    )
    wanted = jnp.concatenate(
        [jnp.broadcast_to(station_ref[k : k + 1, :], (4, count)) for k in range(2)], axis=0
    ).astype(F32)
    wanted = wanted.T
    station = lax.broadcasted_iota(jnp.int32, (count, stations), 1).astype(F32)
    first = dot((station == wanted[:, 0:1]).astype(F32).astype(BF16), screen_pair)
    second = dot((station == wanted[:, 4:5]).astype(F32).astype(BF16), screen_pair)
    first_real, first_imag = first[:, :LANES], first[:, LANES:]
    second_real, second_imag = second[:, :LANES], second[:, LANES:]
    taper = taper_ref[pl.ds(facet, 1), :]
    weight_real = taper * (first_real * second_real + first_imag * second_imag)
    weight_imag = taper * (first_real * second_imag - first_imag * second_real)
    image_real = images[:, 0].reshape(count, LANES)
    image_imag = images[:, 1].reshape(count, LANES)
    weighted = jnp.concatenate(
        [
            weight_real * image_real - weight_imag * image_imag,
            weight_real * image_imag + weight_imag * image_real,
        ],
        axis=1,
    ).astype(BF16)
    mixed[...] = dot(weighted, table_ref[...]).astype(BF16)

    out_copies = []
    for step in range(1, facets):
        copy = pltpu.make_async_remote_copy(
            src_ref=mixed,
            dst_ref=out_ref.at[facet],
            send_sem=out_send.at[step],
            recv_sem=out_recv.at[step],
            device_id={"facet": lax.rem(facet + step, facets)},
            device_id_type=MESH,
        )
        copy.start()
        out_copies.append(copy)
    out_ref[facet] = mixed[...]
    for copy in out_copies:
        copy.wait()


def gather_rows(visibilities, coordinates, screens, stations, facets, times):
    own = visibilities.shape[1]
    count = stations.shape[1]
    vmem = pl.BlockSpec(memory_space=pltpu.VMEM)
    return pl.pallas_call(
        functools.partial(rows_kernel, facets, times),
        out_shape=jax.ShapeDtypeStruct((facets, count, 2 * LANES), BF16),
        in_specs=[vmem] * 6,
        out_specs=vmem,
        scratch_shapes=[
            pltpu.VMEM((5, own, NT), F32),
            pltpu.VMEM((GROUPS, 2, own, LANES), F32),
            pltpu.VMEM((GROUPS, 2, own, LANES), F32),
            pltpu.VMEM((times,) + screens.shape[1:], BF16),
            pltpu.VMEM((count, 2 * LANES), BF16),
            pltpu.SemaphoreType.DMA((facets,)),
            pltpu.SemaphoreType.DMA((facets,)),
            pltpu.SemaphoreType.DMA((times,)),
            pltpu.SemaphoreType.DMA((times,)),
            pltpu.SemaphoreType.DMA((facets,)),
            pltpu.SemaphoreType.DMA((facets,)),
        ],
        compiler_params=pltpu.CompilerParams(collective_id=0, has_side_effects=True),
        name="subgrid_rows",
    )(
        visibilities,
        coordinates,
        screens,
        stations,
        jnp.asarray(taper_table()),
        jnp.asarray(dft_rows_table()),
    )


def eight_point(parts):
    root = math.sqrt(0.5)

    def add(a, b):
        return a[0] + b[0], a[1] + b[1]

    def sub(a, b):
        return a[0] - b[0], a[1] - b[1]

    def minus_i(a):
        return a[1], -a[0]

    def four_point(p):
        even_sum, even_diff = add(p[0], p[2]), sub(p[0], p[2])
        odd_sum, odd_diff = add(p[1], p[3]), minus_i(sub(p[1], p[3]))
        return add(even_sum, odd_sum), add(even_diff, odd_diff), sub(even_sum, odd_sum), sub(even_diff, odd_diff)

    even = four_point(parts[0::2])
    odd = list(four_point(parts[1::2]))
    odd[1] = ((odd[1][0] + odd[1][1]) * root, (odd[1][1] - odd[1][0]) * root)
    odd[2] = minus_i(odd[2])
    odd[3] = ((odd[3][1] - odd[3][0]) * root, -(odd[3][0] + odd[3][1]) * root)
    return [add(even[k], odd[k]) for k in range(4)] + [sub(even[k], odd[k]) for k in range(4)]


def fold_kernel(
    facet_ref,
    corner_smem,
    corner_ref,
    member_ref,
    mixed_ref,
    columns_ref,
    out_ref,
    spread,
    cells,
    folded_real,
    folded_imag,
):
    count = corner_ref.shape[1]
    anchor_x = facet_ref[0] % 4 * (GRID // FP // 4)
    anchor_y = facet_ref[0] // 4 % 4 * (GRID // FP // 4)
    folded = (folded_real, folded_imag)
    for whole in folded:
        whole[...] = jnp.zeros_like(whole)

    rows = 16

    def eight(step, carry):
        at = pl.ds(pl.multiple_of(step * rows, rows), rows)
        parts = []
        for source in range(GROUPS):
            pair = mixed_ref[source, at, :].astype(F32)
            parts.append((pair[:, :LANES], pair[:, LANES:]))
        for a_lo, value in enumerate(eight_point(parts)):
            spread[a_lo, at, :] = jnp.concatenate(value, axis=1).astype(BF16)
        return carry

    lax.fori_loop(0, count // rows, eight, 0)

    phase = (
        (corner_ref[0:1, :] & (GRID - 1)) * anchor_x + (corner_ref[1:2, :] & (GRID - 1)) * anchor_y
    ) & (GRID - 1)
    cos_corner, sin_corner = cos_sin(phase.astype(F32) * (1.0 / GRID))
    member = member_ref[...].astype(F32)
    pair = jnp.concatenate([cos_corner * member] * 4 + [sin_corner * member] * 4, axis=0).T
    cos_corner, sin_corner = pair[:, 0:1], pair[:, 4:5]
    lane = lax.broadcasted_iota(jnp.int32, (GROUPS, LANES), 1)
    low = lax.broadcasted_iota(jnp.int32, (GROUPS, LANES), 0)
    offset = (8 * (lane // S) + low) * anchor_x + lane % S * anchor_y
    cos_cells, sin_cells = cos_sin(offset.astype(F32) * (1.0 / GRID))
    for a_lo in range(GROUPS):
        cos_cell, sin_cell = cos_cells[a_lo : a_lo + 1], sin_cells[a_lo : a_lo + 1]
        value = dot(spread[a_lo], columns_ref[a_lo])
        real, imag = value[:, :LANES], value[:, LANES:]
        cos_all = cos_corner * cos_cell - sin_corner * sin_cell
        sin_all = cos_corner * sin_cell + sin_corner * cos_cell
        cells[pl.ds(a_lo * count, count), :] = real * cos_all - imag * sin_all
        cells[pl.ds((GROUPS + a_lo) * count, count), :] = real * sin_all + imag * cos_all

    lane8 = lax.broadcasted_iota(jnp.int32, (8, LANES), 1)

    def prepare(number):
        first_u = corner_smem[0, number] & (FP - 1)
        first_v = corner_smem[1, number] & (FP - 1)
        tile = first_v // LANES
        within = first_v % LANES
        here = (lane8 >= within) & (lane8 < within + S)
        there = lane8 < within + S - LANES
        pieces = []
        for part in range(2):
            block = cells[pl.ds(part * GROUPS * count + number, GROUPS, stride=count), :]
            for a_hi in range(RADIX):
                moved = pltpu.roll(block, (within - S * a_hi) & (LANES - 1), 1)
                at = pl.ds(first_u + 8 * a_hi, 8)
                pieces.append((folded[part], tile, at, jnp.where(here, moved, 0.0)))
                pieces.append((folded[part], tile + 1, at, jnp.where(there, moved, 0.0)))
        return pieces

    def place(step, carry):
        ready = [prepare(step * UNROLL + k) for k in range(UNROLL)]
        for pieces in ready:
            sums = [ref[tile, at, :] + value for ref, tile, at, value in pieces]
            for (ref, tile, at, _), value in zip(pieces, sums):
                ref[tile, at, :] = value
        return carry

    lax.fori_loop(0, count // UNROLL, place, 0)

    tiles = FP // LANES
    for part, whole in enumerate(folded):
        whole[:, 0:S, :] += whole[:, FP : FP + S, :]
        whole[0, 0:FP, :] += whole[tiles, 0:FP, :]
    for residue in range(4):
        for part, whole in enumerate(folded):
            for tile in range(tiles):
                out_ref[
                    pl.ds((2 * residue + part) * LANES, LANES), pl.ds(tile * LANES, LANES)
                ] = whole[tile, pl.ds(residue, LANES, stride=4), :].astype(BF16)


def fold_facet(facet, corners, members, mixed):
    count = corners.shape[1]
    vmem = pl.BlockSpec(memory_space=pltpu.VMEM)
    smem = pl.BlockSpec(memory_space=pltpu.SMEM)
    return pl.pallas_call(
        fold_kernel,
        out_shape=jax.ShapeDtypeStruct((2 * FP, FP), BF16),
        in_specs=[smem, smem, vmem, vmem, vmem, vmem],
        out_specs=vmem,
        scratch_shapes=[
            pltpu.VMEM((GROUPS, count, 2 * LANES), BF16),
            pltpu.VMEM((2 * GROUPS * count, LANES), F32),
            pltpu.VMEM((FP // LANES + 1, FP + S, LANES), F32),
            pltpu.VMEM((FP // LANES + 1, FP + S, LANES), F32),
        ],
        name="fold_facet",
    )(facet.reshape(1), corners, corners, members, mixed, jnp.asarray(dft_columns_table()))


def sum_kernel(
    scale,
    times,
    folded_ref,
    rows_ref,
    edge_ref,
    out_ref,
    lines,
    pair,
    half,
    whole,
    send,
    recv,
    pair_send,
    pair_recv,
):
    time = lax.axis_index("tm")
    chips = times // 2
    core = lax.rem(time, 2)
    chip = time // 2
    other = time + 1 - 2 * core
    barrier = pltpu.get_barrier_semaphore()
    pl.semaphore_signal(barrier, inc=1, device_id={"tm": other}, device_id_type=MESH)
    for step in range(1, chips):
        target = lax.rem(chip + step, chips) * 2 + core
        pl.semaphore_signal(barrier, inc=1, device_id={"tm": target}, device_id_type=MESH)

    parts, width = lines.shape[0], lines.shape[4] // 2
    rows = lines.shape[3]
    quarter = FP // 4
    exchanges = []
    for part in range(parts):
        at = pl.ds(part * width, width)
        terms = []
        for residue in range(4):
            value = dot(rows_ref[residue], folded_ref[pl.ds(residue * 2 * quarter, 2 * quarter), at])
            terms.append((value[:quarter], value[quarter:]))
        even_sum = [terms[0][k] + terms[2][k] for k in range(2)]
        even_diff = [terms[0][k] - terms[2][k] for k in range(2)]
        odd_sum = [terms[1][k] + terms[3][k] for k in range(2)]
        odd_diff = [terms[3][1] - terms[1][1], terms[1][0] - terms[3][0]]
        results = (
            [even_sum[k] + odd_sum[k] for k in range(2)],
            [even_diff[k] + odd_diff[k] for k in range(2)],
            [even_sum[k] - odd_sum[k] for k in range(2)],
            [even_diff[k] - odd_diff[k] for k in range(2)],
        )
        share = chips // 4
        for block, result in enumerate(results):
            for k in range(2):
                lines[part, pl.ds(block * share, share), :, :, pl.ds(k * width, width)] = (
                    result[k].astype(BF16).reshape(share, 2, rows, width)
                )
        if part == 0:
            pl.semaphore_wait(barrier, chips)
        exchange = pltpu.make_async_remote_copy(
            src_ref=lines.at[part, :, 1 - core],
            dst_ref=pair.at[part],
            send_sem=pair_send.at[part],
            recv_sem=pair_recv.at[part],
            device_id={"tm": other},
            device_id_type=MESH,
        )
        exchange.start()
        exchanges.append(exchange)

    copies = []
    for part in range(parts):
        exchanges[part].wait()
        half[part] = (lines[part, :, core].astype(F32) + pair[part].astype(F32)).astype(BF16)
        for step in range(1, chips):
            target = lax.rem(chip + step, chips)
            copy = pltpu.make_async_remote_copy(
                src_ref=half.at[part, target],
                dst_ref=whole.at[part, chip],
                send_sem=send.at[part, step],
                recv_sem=recv.at[part, step],
                device_id={"tm": target * 2 + core},
                device_id_type=MESH,
            )
            copy.start()
            copies.append(copy)
        whole[part, chip] = half[part, chip]
    for copy in copies:
        copy.wait()
    totals = []
    for part in range(parts):
        total = whole[part, 0].astype(F32)
        for source in range(1, chips):
            total = total + whole[part, source].astype(F32)
        totals.append(total.astype(BF16))
    real = jnp.concatenate([total[:, :width] for total in totals], axis=1)
    imag = jnp.concatenate([total[:, width:] for total in totals], axis=1)
    cos_part, sin_part = edge_ref[:, :FP], edge_ref[:, FP:]
    out_ref[0] = (dot(real, cos_part) - dot(imag, sin_part)) * scale
    out_ref[1] = (dot(real, sin_part) + dot(imag, cos_part)) * scale


def sum_facet(folded, scale, times):
    chips = times // 2
    rows = FP // times
    parts = 2
    width = FP // parts
    vmem = pl.BlockSpec(memory_space=pltpu.VMEM)
    return pl.pallas_call(
        functools.partial(sum_kernel, scale, times),
        out_shape=jax.ShapeDtypeStruct((2, rows, FP), F32),
        in_specs=[vmem] * 3,
        out_specs=vmem,
        scratch_shapes=[
            pltpu.VMEM((parts, chips, 2, rows, 2 * width), BF16),
            pltpu.VMEM((parts, chips, rows, 2 * width), BF16),
            pltpu.VMEM((parts, chips, rows, 2 * width), BF16),
            pltpu.VMEM((parts, chips, rows, 2 * width), BF16),
            pltpu.SemaphoreType.DMA((parts, chips)),
            pltpu.SemaphoreType.DMA((parts, chips)),
            pltpu.SemaphoreType.DMA((parts,)),
            pltpu.SemaphoreType.DMA((parts,)),
        ],
        compiler_params=pltpu.CompilerParams(collective_id=1, has_side_effects=True),
        name="sum_facet",
    )(folded, jnp.asarray(facet_rows_table()), jnp.asarray(facet_table()))


def per_device(
    visibilities, coordinates, station_screens, subgrid_stations, subgrid_corners, facet_member
):
    times = lax.axis_size("tm")
    facets = lax.axis_size("facet")
    facet = lax.axis_index("facet")
    screens = jnp.transpose(
        lax.dynamic_slice_in_dim(station_screens, facet * LANES, LANES, axis=3), (0, 2, 1, 3)
    )
    mixed = gather_rows(
        visibilities, coordinates, screens, jnp.transpose(subgrid_stations), facets, times
    )
    folded = fold_facet(facet, jnp.transpose(subgrid_corners), jnp.transpose(facet_member), mixed)
    total_count = visibilities.shape[1] * facets * times
    scale = 1.0 / (S * math.sqrt(visibilities.shape[2] * total_count))
    own_rows = sum_facet(folded, scale, times)
    return own_rows[:, None]


def solution(mesh):
    in_specs = (
        P(None, ("tm", "facet"), None),
        P(None, ("tm", "facet"), None),
        P(None, "tm", None, None),
        P("tm", None),
        P("tm", None),
        P("tm", "facet"),
    )
    out_specs = P(None, "facet", "tm", None)
    return jax.shard_map(
        per_device, mesh=mesh, in_specs=in_specs, out_specs=out_specs, check_vma=False
    )
```

```python
import functools
import math

import jax
import jax.numpy as jnp
import numpy as np
from jax import lax
from jax.experimental import pallas as pl
from jax.experimental.pallas import tpu as pltpu
from jax.sharding import PartitionSpec as P

UNROLL = 16
GRID = 65536
S = 32
NT = 128
SLABS = 2
FP = 512
LANES = 128
GROUPS = 8
RADIX = 4
MESH = pl.DeviceIdType.MESH
F32 = jnp.float32
BF16 = jnp.bfloat16


def rounded(values):
    return np.asarray(values, np.float32).astype(jnp.bfloat16)


def complex_block(values):
    return np.block([[values.real, values.imag], [-values.imag, values.real]])


def dft_rows_table():
    offsets = np.arange(S) - S // 2
    table = np.exp(-2j * np.pi * (np.outer(offsets, offsets) % S) / S) / math.sqrt(S)
    return rounded(complex_block(np.kron(np.eye(RADIX), table.T)))


def dft_columns_table():
    tables = []
    for a_lo in range(GROUPS):
        offset = 8 * (np.arange(RADIX) - 2) + a_lo
        factor = (-1.0) ** a_lo * np.exp(-2j * np.pi * np.outer(np.arange(RADIX), offset) / S) / math.sqrt(S)
        tables.append(rounded(complex_block(np.kron(factor, np.eye(S)))))
    return np.stack(tables)


def facet_table():
    angles = 2.0 * np.pi * (np.outer(np.arange(FP), np.arange(FP)) % FP) / FP
    return rounded(np.concatenate([np.cos(angles), np.sin(angles)], axis=1))


def facet_rows_table():
    tables = []
    for residue in range(4):
        angles = 2.0 * np.pi * (np.outer(np.arange(FP // 4), np.arange(residue, FP, 4)) % FP) / FP
        tables.append(rounded(complex_block(np.exp(-1j * angles))))
    return np.stack(tables)


def taper_table():
    centre = np.sin(np.pi * (np.arange(S) + 0.5) / S)
    return np.outer(centre, centre).reshape(GROUPS, LANES).astype(np.float32)


def cos_sin(turns):
    rest = turns - jnp.round(turns)
    angle = rest * math.pi
    square = angle * angle
    sin_half = -1.0 / 39916800.0
    for term in (1.0 / 362880.0, -1.0 / 5040.0, 1.0 / 120.0, -1.0 / 6.0, 1.0):
        sin_half = sin_half * square + term
    sin_half = sin_half * angle
    cos_half = 1.0 / 479001600.0
    for term in (-1.0 / 3628800.0, 1.0 / 40320.0, -1.0 / 720.0, 1.0 / 24.0, -0.5, 1.0):
        cos_half = cos_half * square + term
    return 1.0 - 2.0 * sin_half * sin_half, 2.0 * sin_half * cos_half


def dot(left, right):
    return jnp.dot(left, right, preferred_element_type=F32)


def own_images(inputs_ref, image_ref):
    row = lax.broadcasted_iota(jnp.int32, (S, NT), 0)
    cell_left = (RADIX * (row % GROUPS) + row // GROUPS - S // 2).astype(F32) / S
    cell_right = (row - S // 2).astype(F32) / S
    half_left = cell_left * cell_left * 0.5
    half_right = cell_right * cell_right * 0.5
    lane_block = lax.broadcasted_iota(jnp.int32, (GROUPS, LANES), 1) // S

    def one(number, carry):
        vis_real, vis_imag, shift_u, shift_v, shift_w = (
            inputs_ref[part, pl.ds(number, 1), :] for part in range(5)
        )
        cos_left, sin_left = cos_sin(shift_u * cell_left - shift_w * half_left)
        cos_right, sin_right = cos_sin(shift_v * cell_right - shift_w * half_right)
        left = jnp.concatenate(
            [vis_real * cos_left - vis_imag * sin_left, vis_real * sin_left + vis_imag * cos_left], axis=0
        ).astype(BF16)
        right = jnp.concatenate([cos_right] * RADIX + [sin_right] * RADIX, axis=0).astype(BF16)
        product = lax.dot_general(left, right, (((1,), (1,)), ((), ())), preferred_element_type=F32)
        real = product[:S, :LANES] - product[S:, LANES:]
        imag = product[:S, LANES:] + product[S:, :LANES]
        for part, whole in ((0, real), (1, imag)):
            chosen = whole[:GROUPS]
            for block in range(1, RADIX):
                chosen = jnp.where(lane_block == block, whole[GROUPS * block : GROUPS * (block + 1)], chosen)
            for block in range(GROUPS):
                image_ref[block, part, pl.ds(number, 1), :] = chosen[block : block + 1]
        return carry

    lax.fori_loop(0, inputs_ref.shape[1], one, 0)


def far_first(length):
    return sorted(range(1, length), key=lambda step: -min(step, length - step))


def facet_steps(facets):
    steps = [(turn, step) for turn in range(facets // 4) for step in range(4) if turn or step]
    return sorted(steps, key=lambda pair: -(2 * pair[0] + min(pair[1], 4 - pair[1])))


def rows_kernel(
    facets,
    times,
    vis_ref,
    coord_ref,
    screen_ref,
    station_ref,
    taper_ref,
    table_ref,
    out_ref,
    inputs,
    image,
    images,
    screens,
    mixed,
    image_send,
    image_recv,
    screen_send,
    screen_recv,
    relay_send,
    relay_recv,
    out_send,
    out_recv,
):
    facet = lax.axis_index("facet")
    time = lax.axis_index("tm")
    length = times // 4
    core = lax.rem(time, 2)
    side = lax.rem(time // 2, 2)
    place = time // 4

    def at_time(at_place, at_side, at_core):
        return at_place * 4 + at_side * 2 + at_core

    chips = [(step, turn) for step in far_first(length) + [0] for turn in (1, 0)][:-1]
    others = facet_steps(facets)

    def facet_at(step):
        return lax.rem(facet + step[0] * 4, facets) // 4 * 4 + lax.rem(facet + step[1], 4)

    barrier = pltpu.get_barrier_semaphore()
    for step, turn in chips:
        target = at_time(lax.rem(place + step, length), lax.rem(side + turn, 2), core)
        pl.semaphore_signal(barrier, inc=1, device_id={"tm": target}, device_id_type=MESH)
    for step in others:
        pl.semaphore_signal(barrier, inc=1, device_id={"facet": facet_at(step)}, device_id_type=MESH)
    partner = at_time(place, side, 1 - core)
    pl.semaphore_signal(barrier, inc=1, device_id={"tm": partner}, device_id_type=MESH)

    inputs[0:2] = vis_ref[...].astype(F32)
    inputs[2:5] = coord_ref[...].astype(F32)
    own_images(inputs, image)
    pl.semaphore_wait(barrier, len(chips) + len(others) + 1)

    slab = time // (times // SLABS)
    to_partner = pltpu.make_async_remote_copy(
        src_ref=screen_ref.at[slab],
        dst_ref=screens.at[time],
        send_sem=relay_send.at[len(chips)],
        recv_sem=relay_recv.at[len(chips)],
        device_id={"tm": partner},
        device_id_type=MESH,
    )
    to_partner.start()
    screen_copies = []
    for number, (step, turn) in enumerate(chips):
        target = at_time(lax.rem(place + step, length), lax.rem(side + turn, 2), core)
        copy = pltpu.make_async_remote_copy(
            src_ref=screen_ref.at[target // (times // SLABS)],
            dst_ref=screens.at[time],
            send_sem=screen_send.at[number],
            recv_sem=screen_recv.at[number],
            device_id={"tm": target},
            device_id_type=MESH,
        )
        copy.start()
        screen_copies.append(copy)
    image_copies = []
    for number, step in enumerate(others):
        target = facet_at(step)
        copy = pltpu.make_async_remote_copy(
            src_ref=image.at[target],
            dst_ref=images.at[facet],
            send_sem=image_send.at[number],
            recv_sem=image_recv.at[number],
            device_id={"facet": target},
            device_id_type=MESH,
        )
        copy.start()
        image_copies.append(copy)
    screens[time] = screen_ref[slab]
    images[facet] = image[facet]

    relay_copies = [to_partner]
    for number, (step, turn) in enumerate(chips):
        screen_copies[number].wait_recv()
        source = at_time(lax.rem(place + length - step, length), lax.rem(side + turn, 2), core)
        copy = pltpu.make_async_remote_copy(
            src_ref=screens.at[source],
            dst_ref=screens.at[source],
            send_sem=relay_send.at[number],
            recv_sem=relay_recv.at[number],
            device_id={"tm": partner},
            device_id_type=MESH,
        )
        copy.start()
        relay_copies.append(copy)
    for copy in image_copies + relay_copies:
        copy.wait_recv()

    count = station_ref.shape[1]
    stations = screens.shape[0] * screens.shape[2]
    screen_pair = jnp.concatenate(
        [screens[:, 0].reshape(stations, LANES), screens[:, 1].reshape(stations, LANES)], axis=1
    )
    wanted = jnp.concatenate(
        [jnp.broadcast_to(station_ref[k : k + 1, :], (4, count)) for k in range(2)], axis=0
    ).astype(F32)
    wanted = wanted.T
    station = lax.broadcasted_iota(jnp.int32, (count, stations), 1).astype(F32)
    first = dot((station == wanted[:, 0:1]).astype(F32).astype(BF16), screen_pair)
    second = dot((station == wanted[:, 4:5]).astype(F32).astype(BF16), screen_pair)
    first_real, first_imag = first[:, :LANES], first[:, LANES:]
    second_real, second_imag = second[:, :LANES], second[:, LANES:]
    taper = taper_ref[pl.ds(facet, 1), :]
    weight_real = taper * (first_real * second_real + first_imag * second_imag)
    weight_imag = taper * (first_real * second_imag - first_imag * second_real)
    image_real = images[:, 0].reshape(count, LANES)
    image_imag = images[:, 1].reshape(count, LANES)
    weighted = jnp.concatenate(
        [
            weight_real * image_real - weight_imag * image_imag,
            weight_real * image_imag + weight_imag * image_real,
        ],
        axis=1,
    ).astype(BF16)
    mixed[...] = dot(weighted, table_ref[...]).astype(BF16)

    out_copies = []
    for number, step in enumerate(others):
        copy = pltpu.make_async_remote_copy(
            src_ref=mixed,
            dst_ref=out_ref.at[facet],
            send_sem=out_send.at[number],
            recv_sem=out_recv.at[number],
            device_id={"facet": facet_at(step)},
            device_id_type=MESH,
        )
        copy.start()
        out_copies.append(copy)
    out_ref[facet] = mixed[...]
    for copy in screen_copies + image_copies + relay_copies:
        copy.wait_send()
    for copy in out_copies:
        copy.wait()


def gather_rows(visibilities, coordinates, screens, stations, facets, times):
    own = visibilities.shape[1]
    count = stations.shape[1]
    vmem = pl.BlockSpec(memory_space=pltpu.VMEM)
    return pl.pallas_call(
        functools.partial(rows_kernel, facets, times),
        out_shape=jax.ShapeDtypeStruct((facets, count, 2 * LANES), BF16),
        in_specs=[vmem] * 6,
        out_specs=vmem,
        scratch_shapes=[
            pltpu.VMEM((5, own, NT), F32),
            pltpu.VMEM((GROUPS, 2, own, LANES), F32),
            pltpu.VMEM((GROUPS, 2, own, LANES), F32),
            pltpu.VMEM((times,) + screens.shape[1:], BF16),
            pltpu.VMEM((count, 2 * LANES), BF16),
            pltpu.SemaphoreType.DMA((facets,)),
            pltpu.SemaphoreType.DMA((facets,)),
            pltpu.SemaphoreType.DMA((times // 2,)),
            pltpu.SemaphoreType.DMA((times // 2,)),
            pltpu.SemaphoreType.DMA((times // 2,)),
            pltpu.SemaphoreType.DMA((times // 2,)),
            pltpu.SemaphoreType.DMA((facets,)),
            pltpu.SemaphoreType.DMA((facets,)),
        ],
        compiler_params=pltpu.CompilerParams(collective_id=0, has_side_effects=True),
        name="subgrid_rows",
    )(
        visibilities,
        coordinates,
        screens,
        stations,
        jnp.asarray(taper_table()),
        jnp.asarray(dft_rows_table()),
    )


def eight_point(parts):
    root = math.sqrt(0.5)

    def add(a, b):
        return a[0] + b[0], a[1] + b[1]

    def sub(a, b):
        return a[0] - b[0], a[1] - b[1]

    def minus_i(a):
        return a[1], -a[0]

    def four_point(p):
        even_sum, even_diff = add(p[0], p[2]), sub(p[0], p[2])
        odd_sum, odd_diff = add(p[1], p[3]), minus_i(sub(p[1], p[3]))
        return add(even_sum, odd_sum), add(even_diff, odd_diff), sub(even_sum, odd_sum), sub(even_diff, odd_diff)

    even = four_point(parts[0::2])
    odd = list(four_point(parts[1::2]))
    odd[1] = ((odd[1][0] + odd[1][1]) * root, (odd[1][1] - odd[1][0]) * root)
    odd[2] = minus_i(odd[2])
    odd[3] = ((odd[3][1] - odd[3][0]) * root, -(odd[3][0] + odd[3][1]) * root)
    return [add(even[k], odd[k]) for k in range(4)] + [sub(even[k], odd[k]) for k in range(4)]


def fold_kernel(
    facet_ref,
    corner_smem,
    corner_ref,
    member_ref,
    mixed_ref,
    columns_ref,
    out_ref,
    spread,
    cells,
    folded_real,
    folded_imag,
):
    count = corner_ref.shape[1]
    anchor_x = facet_ref[0] % 4 * (GRID // FP // 4)
    anchor_y = facet_ref[0] // 4 % 4 * (GRID // FP // 4)
    folded = (folded_real, folded_imag)
    for whole in folded:
        whole[...] = jnp.zeros_like(whole)

    rows = 16

    def eight(step, carry):
        at = pl.ds(pl.multiple_of(step * rows, rows), rows)
        parts = []
        for source in range(GROUPS):
            pair = mixed_ref[source, at, :].astype(F32)
            parts.append((pair[:, :LANES], pair[:, LANES:]))
        for a_lo, value in enumerate(eight_point(parts)):
            spread[a_lo, at, :] = jnp.concatenate(value, axis=1).astype(BF16)
        return carry

    lax.fori_loop(0, count // rows, eight, 0)

    phase = (
        (corner_ref[0:1, :] & (GRID - 1)) * anchor_x + (corner_ref[1:2, :] & (GRID - 1)) * anchor_y
    ) & (GRID - 1)
    cos_corner, sin_corner = cos_sin(phase.astype(F32) * (1.0 / GRID))
    member = member_ref[...].astype(F32)
    pair = jnp.concatenate([cos_corner * member] * 4 + [sin_corner * member] * 4, axis=0).T
    cos_corner, sin_corner = pair[:, 0:1], pair[:, 4:5]
    lane = lax.broadcasted_iota(jnp.int32, (GROUPS, LANES), 1)
    low = lax.broadcasted_iota(jnp.int32, (GROUPS, LANES), 0)
    offset = (8 * (lane // S) + low) * anchor_x + lane % S * anchor_y
    cos_cells, sin_cells = cos_sin(offset.astype(F32) * (1.0 / GRID))
    for a_lo in range(GROUPS):
        cos_cell, sin_cell = cos_cells[a_lo : a_lo + 1], sin_cells[a_lo : a_lo + 1]
        value = dot(spread[a_lo], columns_ref[a_lo])
        real, imag = value[:, :LANES], value[:, LANES:]
        cos_all = cos_corner * cos_cell - sin_corner * sin_cell
        sin_all = cos_corner * sin_cell + sin_corner * cos_cell
        cells[pl.ds(a_lo * count, count), :] = real * cos_all - imag * sin_all
        cells[pl.ds((GROUPS + a_lo) * count, count), :] = real * sin_all + imag * cos_all

    lane8 = lax.broadcasted_iota(jnp.int32, (8, LANES), 1)

    def prepare(number):
        first_u = corner_smem[0, number] & (FP - 1)
        first_v = corner_smem[1, number] & (FP - 1)
        tile = first_v // LANES
        within = first_v % LANES
        here = (lane8 >= within) & (lane8 < within + S)
        there = lane8 < within + S - LANES
        pieces = []
        for part in range(2):
            block = cells[pl.ds(part * GROUPS * count + number, GROUPS, stride=count), :]
            for a_hi in range(RADIX):
                moved = pltpu.roll(block, (within - S * a_hi) & (LANES - 1), 1)
                at = pl.ds(first_u + 8 * a_hi, 8)
                pieces.append((folded[part], tile, at, jnp.where(here, moved, 0.0)))
                pieces.append((folded[part], tile + 1, at, jnp.where(there, moved, 0.0)))
        return pieces

    def place(step, carry):
        ready = [prepare(step * UNROLL + k) for k in range(UNROLL)]
        for pieces in ready:
            sums = [ref[tile, at, :] + value for ref, tile, at, value in pieces]
            for (ref, tile, at, _), value in zip(pieces, sums):
                ref[tile, at, :] = value
        return carry

    lax.fori_loop(0, count // UNROLL, place, 0)

    tiles = FP // LANES
    for part, whole in enumerate(folded):
        whole[:, 0:S, :] += whole[:, FP : FP + S, :]
        whole[0, 0:FP, :] += whole[tiles, 0:FP, :]
    for residue in range(4):
        for part, whole in enumerate(folded):
            for tile in range(tiles):
                out_ref[
                    pl.ds((2 * residue + part) * LANES, LANES), pl.ds(tile * LANES, LANES)
                ] = whole[tile, pl.ds(residue, LANES, stride=4), :].astype(BF16)


def fold_facet(facet, corners, members, mixed):
    count = corners.shape[1]
    vmem = pl.BlockSpec(memory_space=pltpu.VMEM)
    smem = pl.BlockSpec(memory_space=pltpu.SMEM)
    return pl.pallas_call(
        fold_kernel,
        out_shape=jax.ShapeDtypeStruct((2 * FP, FP), BF16),
        in_specs=[smem, smem, vmem, vmem, vmem, vmem],
        out_specs=vmem,
        scratch_shapes=[
            pltpu.VMEM((GROUPS, count, 2 * LANES), BF16),
            pltpu.VMEM((2 * GROUPS * count, LANES), F32),
            pltpu.VMEM((FP // LANES + 1, FP + S, LANES), F32),
            pltpu.VMEM((FP // LANES + 1, FP + S, LANES), F32),
        ],
        name="fold_facet",
    )(facet.reshape(1), corners, corners, members, mixed, jnp.asarray(dft_columns_table()))


def sum_kernel(
    scale,
    times,
    folded_ref,
    rows_ref,
    edge_ref,
    out_ref,
    lines,
    pair,
    beside_out,
    beside,
    ring_out,
    ring,
    pair_send,
    pair_recv,
    beside_send,
    beside_recv,
    ring_send,
    ring_recv,
):
    time = lax.axis_index("tm")
    length = times // 4
    core = lax.rem(time, 2)
    side = lax.rem(time // 2, 2)
    place = time // 4
    order = far_first(length) + [0]

    def device(at_place, at_side, at_core):
        return {"tm": at_place * 4 + at_side * 2 + at_core}

    barrier = pltpu.get_barrier_semaphore()
    for step in far_first(length):
        pl.semaphore_signal(
            barrier, inc=1, device_id=device(lax.rem(place + step, length), side, core), device_id_type=MESH
        )
    pl.semaphore_signal(barrier, inc=1, device_id=device(place, 1 - side, core), device_id_type=MESH)
    pl.semaphore_signal(barrier, inc=1, device_id=device(place, side, 1 - core), device_id_type=MESH)

    rows = lines.shape[3]
    quarter = FP // 4
    width = 256
    share = length // 4
    for start in range(0, FP, width):
        terms = []
        for residue in range(4):
            value = dot(
                rows_ref[residue], folded_ref[pl.ds(residue * 2 * quarter, 2 * quarter), pl.ds(start, width)]
            )
            terms.append((value[:quarter], value[quarter:]))
        even_sum = [terms[0][k] + terms[2][k] for k in range(2)]
        even_diff = [terms[0][k] - terms[2][k] for k in range(2)]
        odd_sum = [terms[1][k] + terms[3][k] for k in range(2)]
        odd_diff = [terms[3][1] - terms[1][1], terms[1][0] - terms[3][0]]
        results = (
            [even_sum[k] + odd_sum[k] for k in range(2)],
            [even_diff[k] + odd_diff[k] for k in range(2)],
            [even_sum[k] - odd_sum[k] for k in range(2)],
            [even_diff[k] - odd_diff[k] for k in range(2)],
        )
        for block, result in enumerate(results):
            for k in range(2):
                lines[pl.ds(block * share, share), :, :, :, pl.ds(k * FP + start, width)] = (
                    result[k].astype(BF16).reshape(share, 2, 2, rows, width)
                )
    pl.semaphore_wait(barrier, length + 1)

    copies = []
    for step in order:
        target = lax.rem(place + step, length)
        copy = pltpu.make_async_remote_copy(
            src_ref=lines.at[target, :, 1 - core],
            dst_ref=pair.at[target],
            send_sem=pair_send.at[step],
            recv_sem=pair_recv.at[step],
            device_id=device(place, side, 1 - core),
            device_id_type=MESH,
        )
        copy.start()
        copies.append(copy)
    beside_copies = []
    for step, copy in zip(order, copies):
        target = lax.rem(place + step, length)
        copy.wait_recv()
        beside_out[target] = (
            lines[target, 1 - side, core].astype(F32) + pair[target, 1 - side].astype(F32)
        ).astype(BF16)
        onward = pltpu.make_async_remote_copy(
            src_ref=beside_out.at[target],
            dst_ref=beside.at[target],
            send_sem=beside_send.at[step],
            recv_sem=beside_recv.at[step],
            device_id=device(place, 1 - side, core),
            device_id_type=MESH,
        )
        onward.start()
        beside_copies.append(onward)
    ring_copies = []
    for step, copy in zip(order, beside_copies):
        target = lax.rem(place + step, length)
        copy.wait_recv()
        value = (
            lines[target, side, core].astype(F32)
            + pair[target, side].astype(F32)
            + beside[target].astype(F32)
        )
        if step == 0:
            total = value
            continue
        ring_out[target] = value.astype(BF16)
        onward = pltpu.make_async_remote_copy(
            src_ref=ring_out.at[target],
            dst_ref=ring.at[place],
            send_sem=ring_send.at[step],
            recv_sem=ring_recv.at[step],
            device_id=device(target, side, core),
            device_id_type=MESH,
        )
        onward.start()
        ring_copies.append(onward)
    for step, copy in zip(order, ring_copies):
        copy.wait_recv()
        total = total + ring[lax.rem(place + length - step, length)].astype(F32)
    total = total.astype(BF16)
    real, imag = total[:, :FP], total[:, FP:]
    cos_part, sin_part = edge_ref[:, :FP], edge_ref[:, FP:]
    out_ref[0] = (dot(real, cos_part) - dot(imag, sin_part)) * scale
    out_ref[1] = (dot(real, sin_part) + dot(imag, cos_part)) * scale
    for copy in copies + beside_copies + ring_copies:
        copy.wait_send()


def sum_facet(folded, scale, times):
    length = times // 4
    rows = FP // times
    vmem = pl.BlockSpec(memory_space=pltpu.VMEM)
    block = pltpu.VMEM((length, rows, 2 * FP), BF16)
    return pl.pallas_call(
        functools.partial(sum_kernel, scale, times),
        out_shape=jax.ShapeDtypeStruct((2, rows, FP), F32),
        in_specs=[vmem] * 3,
        out_specs=vmem,
        scratch_shapes=[
            pltpu.VMEM((length, 2, 2, rows, 2 * FP), BF16),
            pltpu.VMEM((length, 2, rows, 2 * FP), BF16),
            block,
            block,
            block,
            block,
        ]
        + [pltpu.SemaphoreType.DMA((length,))] * 6,
        compiler_params=pltpu.CompilerParams(collective_id=1, has_side_effects=True),
        name="sum_facet",
    )(folded, jnp.asarray(facet_rows_table()), jnp.asarray(facet_table()))


def per_device(
    visibilities, coordinates, station_screens, subgrid_stations, subgrid_corners, facet_member
):
    times = lax.axis_size("tm")
    facets = lax.axis_size("facet")
    facet = lax.axis_index("facet")
    screens = jnp.transpose(
        lax.dynamic_slice_in_dim(station_screens, facet * LANES, LANES, axis=3), (0, 2, 1, 3)
    )
    mixed = gather_rows(
        visibilities, coordinates, screens, jnp.transpose(subgrid_stations), facets, times
    )
    folded = fold_facet(facet, jnp.transpose(subgrid_corners), jnp.transpose(facet_member), mixed)
    total_count = visibilities.shape[1] * facets * times
    scale = 1.0 / (S * math.sqrt(visibilities.shape[2] * total_count))
    own_rows = sum_facet(folded, scale, times)
    return own_rows[:, None]


def solution(mesh):
    in_specs = (
        P(None, ("tm", "facet"), None),
        P(None, ("tm", "facet"), None),
        P(None, "tm", None, None),
        P("tm", None),
        P("tm", None),
        P("tm", "facet"),
    )
    out_specs = P(None, "facet", "tm", None)
    return jax.shard_map(
        per_device, mesh=mesh, in_specs=in_specs, out_specs=out_specs, check_vma=False
    )
```

```python
import functools
import math

import jax
import jax.numpy as jnp
import numpy as np
from jax import lax
from jax.experimental import pallas as pl
from jax.experimental.pallas import tpu as pltpu
from jax.sharding import PartitionSpec as P

UNROLL = 16
VMEM_LIMIT = 24 * 2**20
GRID = 65536
S = 32
NT = 128
SLABS = 2
FP = 512
LANES = 128
GROUPS = 8
RADIX = 4
MESH = pl.DeviceIdType.MESH
F32 = jnp.float32
BF16 = jnp.bfloat16


def rounded(values):
    return np.asarray(values, np.float32).astype(jnp.bfloat16)


def complex_block(values):
    return np.block([[values.real, values.imag], [-values.imag, values.real]])


def dft_rows_table():
    source = lax.broadcasted_iota(jnp.int32, (LANES, LANES), 0)
    target = lax.broadcasted_iota(jnp.int32, (LANES, LANES), 1)
    phase = (source % S - S // 2) * (target % S - S // 2) & (S - 1)
    cos_part, sin_part = cos_sin(phase.astype(F32) * (1.0 / S))
    same = jnp.where(source // S == target // S, 1.0 / math.sqrt(S), 0.0)
    real, imag = cos_part * same, sin_part * -same
    return jnp.concatenate(
        [jnp.concatenate([real, imag], axis=1), jnp.concatenate([-imag, real], axis=1)], axis=0
    ).astype(BF16)


def dft_columns_table():
    tables = []
    for a_lo in range(GROUPS):
        offset = 8 * (np.arange(RADIX) - 2) + a_lo
        factor = (-1.0) ** a_lo * np.exp(-2j * np.pi * np.outer(np.arange(RADIX), offset) / S) / math.sqrt(S)
        tables.append(rounded(complex_block(np.kron(factor, np.eye(S)))))
    return np.stack(tables)


def facet_table():
    angles = 2.0 * np.pi * (np.outer(np.arange(FP), np.arange(FP)) % FP) / FP
    return rounded(np.concatenate([np.cos(angles), np.sin(angles)], axis=1))


def facet_rows_table():
    tables = []
    for residue in range(4):
        angles = 2.0 * np.pi * (np.outer(np.arange(FP // 4), np.arange(residue, FP, 4)) % FP) / FP
        tables.append(rounded(complex_block(np.exp(-1j * angles))))
    return np.stack(tables)


def cos_sin(turns):
    rest = turns - jnp.round(turns)
    angle = rest * math.pi
    square = angle * angle
    sin_half = -1.0 / 39916800.0
    for term in (1.0 / 362880.0, -1.0 / 5040.0, 1.0 / 120.0, -1.0 / 6.0, 1.0):
        sin_half = sin_half * square + term
    sin_half = sin_half * angle
    cos_half = 1.0 / 479001600.0
    for term in (-1.0 / 3628800.0, 1.0 / 40320.0, -1.0 / 720.0, 1.0 / 24.0, -0.5, 1.0):
        cos_half = cos_half * square + term
    return 1.0 - 2.0 * sin_half * sin_half, 2.0 * sin_half * cos_half


def dot(left, right):
    return jnp.dot(left, right, preferred_element_type=F32)


def own_images(inputs_ref, image_ref):
    row = lax.broadcasted_iota(jnp.int32, (S, NT), 0)
    cell_left = (RADIX * (row % GROUPS) + row // GROUPS - S // 2).astype(F32) / S
    cell_right = (row - S // 2).astype(F32) / S
    half_left = cell_left * cell_left * 0.5
    half_right = cell_right * cell_right * 0.5
    lane_block = lax.broadcasted_iota(jnp.int32, (GROUPS, LANES), 1) // S

    def one(number, carry):
        vis_real, vis_imag, shift_u, shift_v, shift_w = (
            inputs_ref[part, pl.ds(number, 1), :] for part in range(5)
        )
        cos_left, sin_left = cos_sin(shift_u * cell_left - shift_w * half_left)
        cos_right, sin_right = cos_sin(shift_v * cell_right - shift_w * half_right)
        left = jnp.concatenate(
            [vis_real * cos_left - vis_imag * sin_left, vis_real * sin_left + vis_imag * cos_left], axis=0
        ).astype(BF16)
        right = jnp.concatenate([cos_right] * RADIX + [sin_right] * RADIX, axis=0).astype(BF16)
        product = lax.dot_general(left, right, (((1,), (1,)), ((), ())), preferred_element_type=F32)
        real = product[:S, :LANES] - product[S:, LANES:]
        imag = product[:S, LANES:] + product[S:, :LANES]
        for part, whole in ((0, real), (1, imag)):
            chosen = whole[:GROUPS]
            for block in range(1, RADIX):
                chosen = jnp.where(lane_block == block, whole[GROUPS * block : GROUPS * (block + 1)], chosen)
            for block in range(GROUPS):
                image_ref[block, part, pl.ds(number, 1), :] = chosen[block : block + 1]
        return carry

    lax.fori_loop(0, inputs_ref.shape[1], one, 0)


def far_first(length):
    return sorted(range(1, length), key=lambda step: -min(step, length - step))


def facet_steps(facets):
    steps = [(turn, step) for turn in range(facets // 4) for step in range(4) if turn or step]
    return sorted(steps, key=lambda pair: -(2 * pair[0] + min(pair[1], 4 - pair[1])))


def rows_kernel(
    facets,
    times,
    vis_ref,
    coord_ref,
    screen_ref,
    station_ref,
    out_ref,
    inputs,
    image,
    images,
    screens,
    mixed,
    table,
    image_send,
    image_recv,
    screen_send,
    screen_recv,
    relay_send,
    relay_recv,
    out_send,
    out_recv,
):
    facet = lax.axis_index("facet")
    time = lax.axis_index("tm")
    length = times // 4
    core = lax.rem(time, 2)
    side = lax.rem(time // 2, 2)
    place = time // 4

    def at_time(at_place, at_side, at_core):
        return at_place * 4 + at_side * 2 + at_core

    chips = [(step, turn) for step in far_first(length) + [0] for turn in (1, 0)][:-1]
    others = facet_steps(facets)

    def facet_at(step):
        return lax.rem(facet + step[0] * 4, facets) // 4 * 4 + lax.rem(facet + step[1], 4)

    barrier = pltpu.get_barrier_semaphore()
    for step, turn in chips:
        target = at_time(lax.rem(place + step, length), lax.rem(side + turn, 2), core)
        pl.semaphore_signal(barrier, inc=1, device_id={"tm": target}, device_id_type=MESH)
    for step in others:
        pl.semaphore_signal(barrier, inc=1, device_id={"facet": facet_at(step)}, device_id_type=MESH)
    partner = at_time(place, side, 1 - core)
    pl.semaphore_signal(barrier, inc=1, device_id={"tm": partner}, device_id_type=MESH)

    inputs[0:2] = vis_ref[...].astype(F32)
    inputs[2:5] = coord_ref[...].astype(F32)
    own_images(inputs, image)
    pl.semaphore_wait(barrier, len(chips) + len(others) + 1)

    slab = time // (times // SLABS)
    to_partner = pltpu.make_async_remote_copy(
        src_ref=screen_ref.at[slab],
        dst_ref=screens.at[time],
        send_sem=relay_send.at[len(chips)],
        recv_sem=relay_recv.at[len(chips)],
        device_id={"tm": partner},
        device_id_type=MESH,
    )
    to_partner.start()
    screen_copies = []
    for number, (step, turn) in enumerate(chips):
        target = at_time(lax.rem(place + step, length), lax.rem(side + turn, 2), core)
        copy = pltpu.make_async_remote_copy(
            src_ref=screen_ref.at[target // (times // SLABS)],
            dst_ref=screens.at[time],
            send_sem=screen_send.at[number],
            recv_sem=screen_recv.at[number],
            device_id={"tm": target},
            device_id_type=MESH,
        )
        copy.start()
        screen_copies.append(copy)
    image_copies = []
    for number, step in enumerate(others):
        target = facet_at(step)
        copy = pltpu.make_async_remote_copy(
            src_ref=image.at[target],
            dst_ref=images.at[facet],
            send_sem=image_send.at[number],
            recv_sem=image_recv.at[number],
            device_id={"facet": target},
            device_id_type=MESH,
        )
        copy.start()
        image_copies.append(copy)
    screens[time] = screen_ref[slab]
    images[facet] = image[facet]

    table[...] = dft_rows_table()
    relay_copies = [to_partner]
    for number, (step, turn) in enumerate(chips):
        screen_copies[number].wait_recv()
        source = at_time(lax.rem(place + length - step, length), lax.rem(side + turn, 2), core)
        copy = pltpu.make_async_remote_copy(
            src_ref=screens.at[source],
            dst_ref=screens.at[source],
            send_sem=relay_send.at[number],
            recv_sem=relay_recv.at[number],
            device_id={"tm": partner},
            device_id_type=MESH,
        )
        copy.start()
        relay_copies.append(copy)
    for copy in image_copies + relay_copies:
        copy.wait_recv()

    count = station_ref.shape[1]
    stations = screens.shape[0] * screens.shape[2]
    screen_pair = jnp.concatenate(
        [screens[:, 0].reshape(stations, LANES), screens[:, 1].reshape(stations, LANES)], axis=1
    )
    wanted = jnp.concatenate(
        [jnp.broadcast_to(station_ref[k : k + 1, :], (4, count)) for k in range(2)], axis=0
    ).astype(F32)
    wanted = wanted.T
    station = lax.broadcasted_iota(jnp.int32, (count, stations), 1).astype(F32)
    first = dot((station == wanted[:, 0:1]).astype(F32).astype(BF16), screen_pair)
    second = dot((station == wanted[:, 4:5]).astype(F32).astype(BF16), screen_pair)
    first_real, first_imag = first[:, :LANES], first[:, LANES:]
    second_real, second_imag = second[:, :LANES], second[:, LANES:]
    lane = lax.broadcasted_iota(jnp.int32, (GROUPS, LANES), 1)
    _, taper_row = cos_sin((RADIX * facet + lane // S).astype(F32) * (0.5 / S) + 0.25 / S)
    _, taper_column = cos_sin((lane % S).astype(F32) * (0.5 / S) + 0.25 / S)
    taper = (taper_row * taper_column)[0:1]
    weight_real = taper * (first_real * second_real + first_imag * second_imag)
    weight_imag = taper * (first_real * second_imag - first_imag * second_real)
    image_real = images[:, 0].reshape(count, LANES)
    image_imag = images[:, 1].reshape(count, LANES)
    weighted = jnp.concatenate(
        [
            weight_real * image_real - weight_imag * image_imag,
            weight_real * image_imag + weight_imag * image_real,
        ],
        axis=1,
    ).astype(BF16)
    mixed[...] = dot(weighted, table[...]).astype(BF16)

    out_copies = []
    for number, step in enumerate(others):
        copy = pltpu.make_async_remote_copy(
            src_ref=mixed,
            dst_ref=out_ref.at[facet],
            send_sem=out_send.at[number],
            recv_sem=out_recv.at[number],
            device_id={"facet": facet_at(step)},
            device_id_type=MESH,
        )
        copy.start()
        out_copies.append(copy)
    out_ref[facet] = mixed[...]
    for copy in screen_copies + image_copies + relay_copies:
        copy.wait_send()
    for copy in out_copies:
        copy.wait()


def gather_rows(visibilities, coordinates, screens, stations, facets, times):
    own = visibilities.shape[1]
    count = stations.shape[1]
    vmem = pl.BlockSpec(memory_space=pltpu.VMEM)
    return pl.pallas_call(
        functools.partial(rows_kernel, facets, times),
        out_shape=jax.ShapeDtypeStruct((facets, count, 2 * LANES), BF16),
        in_specs=[vmem] * 4,
        out_specs=vmem,
        scratch_shapes=[
            pltpu.VMEM((5, own, NT), F32),
            pltpu.VMEM((GROUPS, 2, own, LANES), F32),
            pltpu.VMEM((GROUPS, 2, own, LANES), F32),
            pltpu.VMEM((times,) + screens.shape[1:], BF16),
            pltpu.VMEM((count, 2 * LANES), BF16),
            pltpu.VMEM((2 * LANES, 2 * LANES), BF16),
            pltpu.SemaphoreType.DMA((facets,)),
            pltpu.SemaphoreType.DMA((facets,)),
            pltpu.SemaphoreType.DMA((times // 2,)),
            pltpu.SemaphoreType.DMA((times // 2,)),
            pltpu.SemaphoreType.DMA((times // 2,)),
            pltpu.SemaphoreType.DMA((times // 2,)),
            pltpu.SemaphoreType.DMA((facets,)),
            pltpu.SemaphoreType.DMA((facets,)),
        ],
        compiler_params=pltpu.CompilerParams(
            collective_id=0, has_side_effects=True, vmem_limit_bytes=VMEM_LIMIT
        ),
        cost_estimate=pl.CostEstimate(flops=2 * 10**9, bytes_accessed=10**7, transcendentals=0),
        name="subgrid_rows",
    )(
        visibilities,
        coordinates,
        screens,
        stations,
    )


def eight_point(parts):
    root = math.sqrt(0.5)

    def add(a, b):
        return a[0] + b[0], a[1] + b[1]

    def sub(a, b):
        return a[0] - b[0], a[1] - b[1]

    def minus_i(a):
        return a[1], -a[0]

    def four_point(p):
        even_sum, even_diff = add(p[0], p[2]), sub(p[0], p[2])
        odd_sum, odd_diff = add(p[1], p[3]), minus_i(sub(p[1], p[3]))
        return add(even_sum, odd_sum), add(even_diff, odd_diff), sub(even_sum, odd_sum), sub(even_diff, odd_diff)

    even = four_point(parts[0::2])
    odd = list(four_point(parts[1::2]))
    odd[1] = ((odd[1][0] + odd[1][1]) * root, (odd[1][1] - odd[1][0]) * root)
    odd[2] = minus_i(odd[2])
    odd[3] = ((odd[3][1] - odd[3][0]) * root, -(odd[3][0] + odd[3][1]) * root)
    return [add(even[k], odd[k]) for k in range(4)] + [sub(even[k], odd[k]) for k in range(4)]


def fold_kernel(
    facet_ref,
    corner_smem,
    corner_ref,
    member_ref,
    mixed_ref,
    columns_ref,
    out_ref,
    spread,
    cells,
    folded_real,
    folded_imag,
):
    count = corner_ref.shape[1]
    anchor_x = facet_ref[0] % 4 * (GRID // FP // 4)
    anchor_y = facet_ref[0] // 4 % 4 * (GRID // FP // 4)
    folded = (folded_real, folded_imag)
    for whole in folded:
        whole[...] = jnp.zeros_like(whole)

    rows = 16

    def eight(step, carry):
        at = pl.ds(pl.multiple_of(step * rows, rows), rows)
        parts = []
        for source in range(GROUPS):
            pair = mixed_ref[source, at, :].astype(F32)
            parts.append((pair[:, :LANES], pair[:, LANES:]))
        for a_lo, value in enumerate(eight_point(parts)):
            spread[a_lo, at, :] = jnp.concatenate(value, axis=1).astype(BF16)
        return carry

    lax.fori_loop(0, count // rows, eight, 0)

    phase = (
        (corner_ref[0:1, :] & (GRID - 1)) * anchor_x + (corner_ref[1:2, :] & (GRID - 1)) * anchor_y
    ) & (GRID - 1)
    cos_corner, sin_corner = cos_sin(phase.astype(F32) * (1.0 / GRID))
    member = member_ref[...].astype(F32)
    pair = jnp.concatenate([cos_corner * member] * 4 + [sin_corner * member] * 4, axis=0).T
    cos_corner, sin_corner = pair[:, 0:1], pair[:, 4:5]
    lane = lax.broadcasted_iota(jnp.int32, (GROUPS, LANES), 1)
    low = lax.broadcasted_iota(jnp.int32, (GROUPS, LANES), 0)
    offset = (8 * (lane // S) + low) * anchor_x + lane % S * anchor_y
    cos_cells, sin_cells = cos_sin(offset.astype(F32) * (1.0 / GRID))
    for a_lo in range(GROUPS):
        cos_cell, sin_cell = cos_cells[a_lo : a_lo + 1], sin_cells[a_lo : a_lo + 1]
        value = dot(spread[a_lo], columns_ref[a_lo])
        real, imag = value[:, :LANES], value[:, LANES:]
        cos_all = cos_corner * cos_cell - sin_corner * sin_cell
        sin_all = cos_corner * sin_cell + sin_corner * cos_cell
        cells[pl.ds(a_lo * count, count), :] = real * cos_all - imag * sin_all
        cells[pl.ds((GROUPS + a_lo) * count, count), :] = real * sin_all + imag * cos_all

    lane8 = lax.broadcasted_iota(jnp.int32, (8, LANES), 1)

    def prepare(number):
        first_u = corner_smem[0, number] & (FP - 1)
        first_v = corner_smem[1, number] & (FP - 1)
        tile = first_v // LANES
        within = first_v % LANES
        here = (lane8 >= within) & (lane8 < within + S)
        there = lane8 < within + S - LANES
        pieces = []
        for part in range(2):
            block = cells[pl.ds(part * GROUPS * count + number, GROUPS, stride=count), :]
            for a_hi in range(RADIX):
                moved = pltpu.roll(block, (within - S * a_hi) & (LANES - 1), 1)
                at = pl.ds(first_u + 8 * a_hi, 8)
                pieces.append((folded[part], tile, at, jnp.where(here, moved, 0.0)))
                pieces.append((folded[part], tile + 1, at, jnp.where(there, moved, 0.0)))
        return pieces

    def place(step, carry):
        ready = [prepare(step * UNROLL + k) for k in range(UNROLL)]
        for pieces in ready:
            sums = [ref[tile, at, :] + value for ref, tile, at, value in pieces]
            for (ref, tile, at, _), value in zip(pieces, sums):
                ref[tile, at, :] = value
        return carry

    lax.fori_loop(0, count // UNROLL, place, 0)

    tiles = FP // LANES
    for part, whole in enumerate(folded):
        whole[:, 0:S, :] += whole[:, FP : FP + S, :]
        whole[0, 0:FP, :] += whole[tiles, 0:FP, :]
    for residue in range(4):
        for part, whole in enumerate(folded):
            for tile in range(tiles):
                out_ref[
                    pl.ds((2 * residue + part) * LANES, LANES), pl.ds(tile * LANES, LANES)
                ] = whole[tile, pl.ds(residue, LANES, stride=4), :].astype(BF16)


def fold_facet(facet, corners, members, mixed):
    count = corners.shape[1]
    vmem = pl.BlockSpec(memory_space=pltpu.VMEM)
    smem = pl.BlockSpec(memory_space=pltpu.SMEM)
    return pl.pallas_call(
        fold_kernel,
        out_shape=jax.ShapeDtypeStruct((2 * FP, FP), BF16),
        in_specs=[smem, smem, vmem, vmem, vmem, vmem],
        out_specs=vmem,
        scratch_shapes=[
            pltpu.VMEM((GROUPS, count, 2 * LANES), BF16),
            pltpu.VMEM((2 * GROUPS * count, LANES), F32),
            pltpu.VMEM((FP // LANES + 1, FP + S, LANES), F32),
            pltpu.VMEM((FP // LANES + 1, FP + S, LANES), F32),
        ],
        compiler_params=pltpu.CompilerParams(vmem_limit_bytes=VMEM_LIMIT),
        name="fold_facet",
    )(facet.reshape(1), corners, corners, members, mixed, jnp.asarray(dft_columns_table()))


def sum_kernel(
    scale,
    times,
    folded_ref,
    rows_ref,
    edge_ref,
    out_ref,
    lines,
    pair,
    beside_out,
    beside,
    ring_out,
    ring,
    pair_send,
    pair_recv,
    beside_send,
    beside_recv,
    ring_send,
    ring_recv,
):
    time = lax.axis_index("tm")
    length = times // 4
    core = lax.rem(time, 2)
    side = lax.rem(time // 2, 2)
    place = time // 4
    order = far_first(length) + [0]

    def device(at_place, at_side, at_core):
        return {"tm": at_place * 4 + at_side * 2 + at_core}

    barrier = pltpu.get_barrier_semaphore()
    for step in far_first(length):
        pl.semaphore_signal(
            barrier, inc=1, device_id=device(lax.rem(place + step, length), side, core), device_id_type=MESH
        )
    pl.semaphore_signal(barrier, inc=1, device_id=device(place, 1 - side, core), device_id_type=MESH)
    pl.semaphore_signal(barrier, inc=1, device_id=device(place, side, 1 - core), device_id_type=MESH)

    rows = lines.shape[3]
    quarter = FP // 4
    width = 256
    share = length // 4
    for start in range(0, FP, width):
        terms = []
        for residue in range(4):
            value = dot(
                rows_ref[residue], folded_ref[pl.ds(residue * 2 * quarter, 2 * quarter), pl.ds(start, width)]
            )
            terms.append((value[:quarter], value[quarter:]))
        even_sum = [terms[0][k] + terms[2][k] for k in range(2)]
        even_diff = [terms[0][k] - terms[2][k] for k in range(2)]
        odd_sum = [terms[1][k] + terms[3][k] for k in range(2)]
        odd_diff = [terms[3][1] - terms[1][1], terms[1][0] - terms[3][0]]
        results = (
            [even_sum[k] + odd_sum[k] for k in range(2)],
            [even_diff[k] + odd_diff[k] for k in range(2)],
            [even_sum[k] - odd_sum[k] for k in range(2)],
            [even_diff[k] - odd_diff[k] for k in range(2)],
        )
        for block, result in enumerate(results):
            for k in range(2):
                lines[pl.ds(block * share, share), :, :, :, pl.ds(k * FP + start, width)] = (
                    result[k].astype(BF16).reshape(share, 2, 2, rows, width)
                )
    pl.semaphore_wait(barrier, length + 1)

    copies = []
    for step in order:
        target = lax.rem(place + step, length)
        copy = pltpu.make_async_remote_copy(
            src_ref=lines.at[target, :, 1 - core],
            dst_ref=pair.at[target],
            send_sem=pair_send.at[step],
            recv_sem=pair_recv.at[step],
            device_id=device(place, side, 1 - core),
            device_id_type=MESH,
        )
        copy.start()
        copies.append(copy)
    beside_copies = []
    for step, copy in zip(order, copies):
        target = lax.rem(place + step, length)
        copy.wait_recv()
        beside_out[target] = (
            lines[target, 1 - side, core].astype(F32) + pair[target, 1 - side].astype(F32)
        ).astype(BF16)
        onward = pltpu.make_async_remote_copy(
            src_ref=beside_out.at[target],
            dst_ref=beside.at[target],
            send_sem=beside_send.at[step],
            recv_sem=beside_recv.at[step],
            device_id=device(place, 1 - side, core),
            device_id_type=MESH,
        )
        onward.start()
        beside_copies.append(onward)
    ring_copies = []
    for step, copy in zip(order, beside_copies):
        target = lax.rem(place + step, length)
        copy.wait_recv()
        value = (
            lines[target, side, core].astype(F32)
            + pair[target, side].astype(F32)
            + beside[target].astype(F32)
        )
        if step == 0:
            total = value
            continue
        ring_out[target] = value.astype(BF16)
        onward = pltpu.make_async_remote_copy(
            src_ref=ring_out.at[target],
            dst_ref=ring.at[place],
            send_sem=ring_send.at[step],
            recv_sem=ring_recv.at[step],
            device_id=device(target, side, core),
            device_id_type=MESH,
        )
        onward.start()
        ring_copies.append(onward)
    for step, copy in zip(order, ring_copies):
        copy.wait_recv()
        total = total + ring[lax.rem(place + length - step, length)].astype(F32)
    total = total.astype(BF16)
    real, imag = total[:, :FP], total[:, FP:]
    cos_part, sin_part = edge_ref[:, :FP], edge_ref[:, FP:]
    out_ref[0] = (dot(real, cos_part) - dot(imag, sin_part)) * scale
    out_ref[1] = (dot(real, sin_part) + dot(imag, cos_part)) * scale
    for copy in copies + beside_copies + ring_copies:
        copy.wait_send()


def sum_facet(folded, scale, times):
    length = times // 4
    rows = FP // times
    vmem = pl.BlockSpec(memory_space=pltpu.VMEM)
    block = pltpu.VMEM((length, rows, 2 * FP), BF16)
    return pl.pallas_call(
        functools.partial(sum_kernel, scale, times),
        out_shape=jax.ShapeDtypeStruct((2, rows, FP), F32),
        in_specs=[vmem] * 3,
        out_specs=vmem,
        scratch_shapes=[
            pltpu.VMEM((length, 2, 2, rows, 2 * FP), BF16),
            pltpu.VMEM((length, 2, rows, 2 * FP), BF16),
            block,
            block,
            block,
            block,
        ]
        + [pltpu.SemaphoreType.DMA((length,))] * 6,
        compiler_params=pltpu.CompilerParams(
            collective_id=1, has_side_effects=True, vmem_limit_bytes=VMEM_LIMIT
        ),
        name="sum_facet",
    )(folded, jnp.asarray(facet_rows_table()), jnp.asarray(facet_table()))


def per_device(
    visibilities, coordinates, station_screens, subgrid_stations, subgrid_corners, facet_member
):
    times = lax.axis_size("tm")
    facets = lax.axis_size("facet")
    facet = lax.axis_index("facet")
    screens = jnp.transpose(
        lax.dynamic_slice_in_dim(station_screens, facet * LANES, LANES, axis=3), (0, 2, 1, 3)
    )
    mixed = gather_rows(
        visibilities, coordinates, screens, jnp.transpose(subgrid_stations), facets, times
    )
    folded = fold_facet(facet, jnp.transpose(subgrid_corners), jnp.transpose(facet_member), mixed)
    total_count = visibilities.shape[1] * facets * times
    scale = 1.0 / (S * math.sqrt(visibilities.shape[2] * total_count))
    own_rows = sum_facet(folded, scale, times)
    return own_rows[:, None]


def solution(mesh):
    in_specs = (
        P(None, ("tm", "facet"), None),
        P(None, ("tm", "facet"), None),
        P(None, "tm", None, None),
        P("tm", None),
        P("tm", None),
        P("tm", "facet"),
    )
    out_specs = P(None, "facet", "tm", None)
    return jax.shard_map(
        per_device, mesh=mesh, in_specs=in_specs, out_specs=out_specs, check_vma=False
    )
```

```python
import functools
import math

import jax
import jax.numpy as jnp
import numpy as np
from jax import lax
from jax.experimental import pallas as pl
from jax.experimental.pallas import tpu as pltpu
from jax.sharding import PartitionSpec as P

UNROLL = 32
VMEM_LIMIT = 24 * 2**20
GRID = 65536
S = 32
NT = 128
SLABS = 2
FP = 512
LANES = 128
GROUPS = 8
RADIX = 4
MESH = pl.DeviceIdType.MESH
F32 = jnp.float32
BF16 = jnp.bfloat16


def rounded(values):
    return np.asarray(values, np.float32).astype(jnp.bfloat16)


def complex_block(values):
    return np.block([[values.real, values.imag], [-values.imag, values.real]])


def dft_rows_table():
    source = lax.broadcasted_iota(jnp.int32, (LANES, LANES), 0)
    target = lax.broadcasted_iota(jnp.int32, (LANES, LANES), 1)
    phase = (source % S - S // 2) * (target % S - S // 2) & (S - 1)
    cos_part, sin_part = cos_sin(phase.astype(F32) * (1.0 / S))
    same = jnp.where(source // S == target // S, 1.0 / math.sqrt(S), 0.0)
    real, imag = cos_part * same, sin_part * -same
    return jnp.concatenate(
        [jnp.concatenate([real, imag], axis=1), jnp.concatenate([-imag, real], axis=1)], axis=0
    ).astype(BF16)


def dft_columns_table():
    tables = []
    for a_lo in range(GROUPS):
        offset = 8 * (np.arange(RADIX) - 2) + a_lo
        factor = (-1.0) ** a_lo * np.exp(-2j * np.pi * np.outer(np.arange(RADIX), offset) / S) / math.sqrt(S)
        tables.append(rounded(complex_block(np.kron(factor, np.eye(S)))))
    return np.stack(tables)


def facet_table():
    angles = 2.0 * np.pi * (np.outer(np.arange(FP), np.arange(FP)) % FP) / FP
    return rounded(np.concatenate([np.cos(angles), np.sin(angles)], axis=1))


def facet_rows_table():
    tables = []
    for residue in range(4):
        angles = 2.0 * np.pi * (np.outer(np.arange(FP // 4), np.arange(residue, FP, 4)) % FP) / FP
        tables.append(rounded(complex_block(np.exp(-1j * angles))))
    return np.stack(tables)


def cos_sin(turns):
    rest = turns - jnp.round(turns)
    angle = rest * math.pi
    square = angle * angle
    sin_half = -1.0 / 39916800.0
    for term in (1.0 / 362880.0, -1.0 / 5040.0, 1.0 / 120.0, -1.0 / 6.0, 1.0):
        sin_half = sin_half * square + term
    sin_half = sin_half * angle
    cos_half = 1.0 / 479001600.0
    for term in (-1.0 / 3628800.0, 1.0 / 40320.0, -1.0 / 720.0, 1.0 / 24.0, -0.5, 1.0):
        cos_half = cos_half * square + term
    return 1.0 - 2.0 * sin_half * sin_half, 2.0 * sin_half * cos_half


def dot(left, right):
    return jnp.dot(left, right, preferred_element_type=F32)


def own_images(inputs_ref, image_ref):
    row = lax.broadcasted_iota(jnp.int32, (S, NT), 0)
    cell_left = (RADIX * (row % GROUPS) + row // GROUPS - S // 2).astype(F32) / S
    cell_right = (row - S // 2).astype(F32) / S
    half_left = cell_left * cell_left * 0.5
    half_right = cell_right * cell_right * 0.5
    lane_block = lax.broadcasted_iota(jnp.int32, (GROUPS, LANES), 1) // S

    def one(number, carry):
        vis_real, vis_imag, shift_u, shift_v, shift_w = (
            inputs_ref[part, pl.ds(number, 1), :] for part in range(5)
        )
        cos_left, sin_left = cos_sin(shift_u * cell_left - shift_w * half_left)
        cos_right, sin_right = cos_sin(shift_v * cell_right - shift_w * half_right)
        left = jnp.concatenate(
            [vis_real * cos_left - vis_imag * sin_left, vis_real * sin_left + vis_imag * cos_left], axis=0
        ).astype(BF16)
        right = jnp.concatenate([cos_right] * RADIX + [sin_right] * RADIX, axis=0).astype(BF16)
        product = lax.dot_general(left, right, (((1,), (1,)), ((), ())), preferred_element_type=F32)
        real = product[:S, :LANES] - product[S:, LANES:]
        imag = product[:S, LANES:] + product[S:, :LANES]
        for part, whole in ((0, real), (1, imag)):
            chosen = whole[:GROUPS]
            for block in range(1, RADIX):
                chosen = jnp.where(lane_block == block, whole[GROUPS * block : GROUPS * (block + 1)], chosen)
            for block in range(GROUPS):
                image_ref[block, part, pl.ds(number, 1), :] = chosen[block : block + 1]
        return carry

    lax.fori_loop(0, inputs_ref.shape[1], one, 0)


def far_first(length):
    return sorted(range(1, length), key=lambda step: -min(step, length - step))


def facet_steps(facets):
    steps = [(turn, step) for turn in range(facets // 4) for step in range(4) if turn or step]
    return sorted(steps, key=lambda pair: -(2 * pair[0] + min(pair[1], 4 - pair[1])))


def rows_kernel(
    facets,
    times,
    vis_ref,
    coord_ref,
    screen_ref,
    station_ref,
    out_ref,
    inputs,
    image,
    images,
    screens,
    mixed,
    table,
    image_send,
    image_recv,
    screen_send,
    screen_recv,
    relay_send,
    relay_recv,
    out_send,
    out_recv,
):
    facet = lax.axis_index("facet")
    time = lax.axis_index("tm")
    length = times // 4
    core = lax.rem(time, 2)
    side = lax.rem(time // 2, 2)
    place = time // 4

    def at_time(at_place, at_side, at_core):
        return at_place * 4 + at_side * 2 + at_core

    chips = [(step, turn) for step in far_first(length) + [0] for turn in (1, 0)][:-1]
    others = facet_steps(facets)

    def facet_at(step):
        return lax.rem(facet + step[0] * 4, facets) // 4 * 4 + lax.rem(facet + step[1], 4)

    barrier = pltpu.get_barrier_semaphore()
    for step, turn in chips:
        target = at_time(lax.rem(place + step, length), lax.rem(side + turn, 2), core)
        pl.semaphore_signal(barrier, inc=1, device_id={"tm": target}, device_id_type=MESH)
    for step in others:
        pl.semaphore_signal(barrier, inc=1, device_id={"facet": facet_at(step)}, device_id_type=MESH)
    partner = at_time(place, side, 1 - core)
    pl.semaphore_signal(barrier, inc=1, device_id={"tm": partner}, device_id_type=MESH)

    inputs[0:2] = vis_ref[...].astype(F32)
    inputs[2:5] = coord_ref[...].astype(F32)
    own_images(inputs, image)
    pl.semaphore_wait(barrier, len(chips) + len(others) + 1)

    slab = time // (times // SLABS)
    to_partner = pltpu.make_async_remote_copy(
        src_ref=screen_ref.at[slab],
        dst_ref=screens.at[time],
        send_sem=relay_send.at[len(chips)],
        recv_sem=relay_recv.at[len(chips)],
        device_id={"tm": partner},
        device_id_type=MESH,
    )
    to_partner.start()
    screen_copies = []
    for number, (step, turn) in enumerate(chips):
        target = at_time(lax.rem(place + step, length), lax.rem(side + turn, 2), core)
        copy = pltpu.make_async_remote_copy(
            src_ref=screen_ref.at[target // (times // SLABS)],
            dst_ref=screens.at[time],
            send_sem=screen_send.at[number],
            recv_sem=screen_recv.at[number],
            device_id={"tm": target},
            device_id_type=MESH,
        )
        copy.start()
        screen_copies.append(copy)
    image_copies = []
    for number, step in enumerate(others):
        target = facet_at(step)
        copy = pltpu.make_async_remote_copy(
            src_ref=image.at[target],
            dst_ref=images.at[facet],
            send_sem=image_send.at[number],
            recv_sem=image_recv.at[number],
            device_id={"facet": target},
            device_id_type=MESH,
        )
        copy.start()
        image_copies.append(copy)
    screens[time] = screen_ref[slab]
    images[facet] = image[facet]

    table[...] = dft_rows_table()
    relay_copies = [to_partner]
    for number, (step, turn) in enumerate(chips):
        screen_copies[number].wait_recv()
        source = at_time(lax.rem(place + length - step, length), lax.rem(side + turn, 2), core)
        copy = pltpu.make_async_remote_copy(
            src_ref=screens.at[source],
            dst_ref=screens.at[source],
            send_sem=relay_send.at[number],
            recv_sem=relay_recv.at[number],
            device_id={"tm": partner},
            device_id_type=MESH,
        )
        copy.start()
        relay_copies.append(copy)
    for copy in image_copies + relay_copies:
        copy.wait_recv()

    count = station_ref.shape[1]
    stations = screens.shape[0] * screens.shape[2]
    screen_pair = jnp.concatenate(
        [screens[:, 0].reshape(stations, LANES), screens[:, 1].reshape(stations, LANES)], axis=1
    )
    wanted = jnp.concatenate(
        [jnp.broadcast_to(station_ref[k : k + 1, :], (4, count)) for k in range(2)], axis=0
    ).astype(F32)
    wanted = wanted.T
    station = lax.broadcasted_iota(jnp.int32, (count, stations), 1).astype(F32)
    first = dot((station == wanted[:, 0:1]).astype(F32).astype(BF16), screen_pair)
    second = dot((station == wanted[:, 4:5]).astype(F32).astype(BF16), screen_pair)
    first_real, first_imag = first[:, :LANES], first[:, LANES:]
    second_real, second_imag = second[:, :LANES], second[:, LANES:]
    lane = lax.broadcasted_iota(jnp.int32, (GROUPS, LANES), 1)
    _, taper_row = cos_sin((RADIX * facet + lane // S).astype(F32) * (0.5 / S) + 0.25 / S)
    _, taper_column = cos_sin((lane % S).astype(F32) * (0.5 / S) + 0.25 / S)
    taper = (taper_row * taper_column)[0:1]
    weight_real = taper * (first_real * second_real + first_imag * second_imag)
    weight_imag = taper * (first_real * second_imag - first_imag * second_real)
    image_real = images[:, 0].reshape(count, LANES)
    image_imag = images[:, 1].reshape(count, LANES)
    weighted = jnp.concatenate(
        [
            weight_real * image_real - weight_imag * image_imag,
            weight_real * image_imag + weight_imag * image_real,
        ],
        axis=1,
    ).astype(BF16)
    mixed[...] = dot(weighted, table[...]).astype(BF16)

    out_copies = []
    for number, step in enumerate(others):
        copy = pltpu.make_async_remote_copy(
            src_ref=mixed,
            dst_ref=out_ref.at[facet],
            send_sem=out_send.at[number],
            recv_sem=out_recv.at[number],
            device_id={"facet": facet_at(step)},
            device_id_type=MESH,
        )
        copy.start()
        out_copies.append(copy)
    out_ref[facet] = mixed[...]
    for copy in screen_copies + image_copies + relay_copies:
        copy.wait_send()
    for copy in out_copies:
        copy.wait()


def gather_rows(visibilities, coordinates, screens, stations, facets, times):
    own = visibilities.shape[1]
    count = stations.shape[1]
    vmem = pl.BlockSpec(memory_space=pltpu.VMEM)
    return pl.pallas_call(
        functools.partial(rows_kernel, facets, times),
        out_shape=jax.ShapeDtypeStruct((facets, count, 2 * LANES), BF16),
        in_specs=[vmem] * 4,
        out_specs=vmem,
        scratch_shapes=[
            pltpu.VMEM((5, own, NT), F32),
            pltpu.VMEM((GROUPS, 2, own, LANES), F32),
            pltpu.VMEM((GROUPS, 2, own, LANES), F32),
            pltpu.VMEM((times,) + screens.shape[1:], BF16),
            pltpu.VMEM((count, 2 * LANES), BF16),
            pltpu.VMEM((2 * LANES, 2 * LANES), BF16),
            pltpu.SemaphoreType.DMA((facets,)),
            pltpu.SemaphoreType.DMA((facets,)),
            pltpu.SemaphoreType.DMA((times // 2,)),
            pltpu.SemaphoreType.DMA((times // 2,)),
            pltpu.SemaphoreType.DMA((times // 2,)),
            pltpu.SemaphoreType.DMA((times // 2,)),
            pltpu.SemaphoreType.DMA((facets,)),
            pltpu.SemaphoreType.DMA((facets,)),
        ],
        compiler_params=pltpu.CompilerParams(
            collective_id=0, has_side_effects=True, vmem_limit_bytes=VMEM_LIMIT
        ),
        cost_estimate=pl.CostEstimate(flops=2 * 10**9, bytes_accessed=10**7, transcendentals=0),
        name="subgrid_rows",
    )(
        visibilities,
        coordinates,
        screens,
        stations,
    )


def eight_point(parts):
    root = math.sqrt(0.5)

    def add(a, b):
        return a[0] + b[0], a[1] + b[1]

    def sub(a, b):
        return a[0] - b[0], a[1] - b[1]

    def minus_i(a):
        return a[1], -a[0]

    def four_point(p):
        even_sum, even_diff = add(p[0], p[2]), sub(p[0], p[2])
        odd_sum, odd_diff = add(p[1], p[3]), minus_i(sub(p[1], p[3]))
        return add(even_sum, odd_sum), add(even_diff, odd_diff), sub(even_sum, odd_sum), sub(even_diff, odd_diff)

    even = four_point(parts[0::2])
    odd = list(four_point(parts[1::2]))
    odd[1] = ((odd[1][0] + odd[1][1]) * root, (odd[1][1] - odd[1][0]) * root)
    odd[2] = minus_i(odd[2])
    odd[3] = ((odd[3][1] - odd[3][0]) * root, -(odd[3][0] + odd[3][1]) * root)
    return [add(even[k], odd[k]) for k in range(4)] + [sub(even[k], odd[k]) for k in range(4)]


def fold_kernel(
    facet_ref,
    corner_smem,
    corner_ref,
    member_ref,
    mixed_ref,
    columns_ref,
    out_ref,
    spread,
    cells,
    folded_real,
    folded_imag,
):
    count = corner_ref.shape[1]
    anchor_x = facet_ref[0] % 4 * (GRID // FP // 4)
    anchor_y = facet_ref[0] // 4 % 4 * (GRID // FP // 4)
    folded = (folded_real, folded_imag)
    for whole in folded:
        whole[...] = jnp.zeros_like(whole)

    rows = 16

    def eight(step, carry):
        at = pl.ds(pl.multiple_of(step * rows, rows), rows)
        parts = []
        for source in range(GROUPS):
            pair = mixed_ref[source, at, :].astype(F32)
            parts.append((pair[:, :LANES], pair[:, LANES:]))
        for a_lo, value in enumerate(eight_point(parts)):
            spread[a_lo, at, :] = jnp.concatenate(value, axis=1).astype(BF16)
        return carry

    lax.fori_loop(0, count // rows, eight, 0)

    phase = (
        (corner_ref[0:1, :] & (GRID - 1)) * anchor_x + (corner_ref[1:2, :] & (GRID - 1)) * anchor_y
    ) & (GRID - 1)
    cos_corner, sin_corner = cos_sin(phase.astype(F32) * (1.0 / GRID))
    member = member_ref[...].astype(F32)
    pair = jnp.concatenate([cos_corner * member] * 4 + [sin_corner * member] * 4, axis=0).T
    cos_corner, sin_corner = pair[:, 0:1], pair[:, 4:5]
    lane = lax.broadcasted_iota(jnp.int32, (GROUPS, LANES), 1)
    low = lax.broadcasted_iota(jnp.int32, (GROUPS, LANES), 0)
    offset = (8 * (lane // S) + low) * anchor_x + lane % S * anchor_y
    cos_cells, sin_cells = cos_sin(offset.astype(F32) * (1.0 / GRID))
    for a_lo in range(GROUPS):
        cos_cell, sin_cell = cos_cells[a_lo : a_lo + 1], sin_cells[a_lo : a_lo + 1]
        value = dot(spread[a_lo], columns_ref[a_lo])
        real, imag = value[:, :LANES], value[:, LANES:]
        cos_all = cos_corner * cos_cell - sin_corner * sin_cell
        sin_all = cos_corner * sin_cell + sin_corner * cos_cell
        cells[pl.ds(a_lo * count, count), :] = real * cos_all - imag * sin_all
        cells[pl.ds((GROUPS + a_lo) * count, count), :] = real * sin_all + imag * cos_all

    lane8 = lax.broadcasted_iota(jnp.int32, (8, LANES), 1)

    def prepare(number):
        first_u = corner_smem[0, number] & (FP - 1)
        first_v = corner_smem[1, number] & (FP - 1)
        tile = first_v // LANES
        within = first_v % LANES
        here = (lane8 >= within) & (lane8 < within + S)
        there = lane8 < within + S - LANES
        pieces = []
        for part in range(2):
            block = cells[pl.ds(part * GROUPS * count + number, GROUPS, stride=count), :]
            for a_hi in range(RADIX):
                moved = pltpu.roll(block, (within - S * a_hi) & (LANES - 1), 1)
                at = pl.ds(first_u + 8 * a_hi, 8)
                pieces.append((folded[part], tile, at, jnp.where(here, moved, 0.0)))
                pieces.append((folded[part], tile + 1, at, jnp.where(there, moved, 0.0)))
        return pieces

    def place(step, carry):
        ready = [prepare(step * UNROLL + k) for k in range(UNROLL)]
        for pieces in ready:
            sums = [ref[tile, at, :] + value for ref, tile, at, value in pieces]
            for (ref, tile, at, _), value in zip(pieces, sums):
                ref[tile, at, :] = value
        return carry

    lax.fori_loop(0, count // UNROLL, place, 0)

    tiles = FP // LANES
    for part, whole in enumerate(folded):
        whole[:, 0:S, :] += whole[:, FP : FP + S, :]
        whole[0, 0:FP, :] += whole[tiles, 0:FP, :]
    for residue in range(4):
        for part, whole in enumerate(folded):
            for tile in range(tiles):
                out_ref[
                    pl.ds((2 * residue + part) * LANES, LANES), pl.ds(tile * LANES, LANES)
                ] = whole[tile, pl.ds(residue, LANES, stride=4), :].astype(BF16)


def fold_facet(facet, corners, members, mixed):
    count = corners.shape[1]
    vmem = pl.BlockSpec(memory_space=pltpu.VMEM)
    smem = pl.BlockSpec(memory_space=pltpu.SMEM)
    return pl.pallas_call(
        fold_kernel,
        out_shape=jax.ShapeDtypeStruct((2 * FP, FP), BF16),
        in_specs=[smem, smem, vmem, vmem, vmem, vmem],
        out_specs=vmem,
        scratch_shapes=[
            pltpu.VMEM((GROUPS, count, 2 * LANES), BF16),
            pltpu.VMEM((2 * GROUPS * count, LANES), F32),
            pltpu.VMEM((FP // LANES + 1, FP + S, LANES), F32),
            pltpu.VMEM((FP // LANES + 1, FP + S, LANES), F32),
        ],
        compiler_params=pltpu.CompilerParams(vmem_limit_bytes=VMEM_LIMIT),
        name="fold_facet",
    )(facet.reshape(1), corners, corners, members, mixed, jnp.asarray(dft_columns_table()))


def sum_kernel(
    scale,
    times,
    folded_ref,
    rows_ref,
    edge_ref,
    out_ref,
    lines,
    pair,
    beside_out,
    beside,
    ring_out,
    ring,
    pair_send,
    pair_recv,
    beside_send,
    beside_recv,
    ring_send,
    ring_recv,
):
    time = lax.axis_index("tm")
    length = times // 4
    core = lax.rem(time, 2)
    side = lax.rem(time // 2, 2)
    place = time // 4
    order = far_first(length) + [0]

    def device(at_place, at_side, at_core):
        return {"tm": at_place * 4 + at_side * 2 + at_core}

    barrier = pltpu.get_barrier_semaphore()
    for step in far_first(length):
        pl.semaphore_signal(
            barrier, inc=1, device_id=device(lax.rem(place + step, length), side, core), device_id_type=MESH
        )
    pl.semaphore_signal(barrier, inc=1, device_id=device(place, 1 - side, core), device_id_type=MESH)
    pl.semaphore_signal(barrier, inc=1, device_id=device(place, side, 1 - core), device_id_type=MESH)

    rows = lines.shape[3]
    quarter = FP // 4
    width = 256
    share = length // 4
    for start in range(0, FP, width):
        terms = []
        for residue in range(4):
            value = dot(
                rows_ref[residue], folded_ref[pl.ds(residue * 2 * quarter, 2 * quarter), pl.ds(start, width)]
            )
            terms.append((value[:quarter], value[quarter:]))
        even_sum = [terms[0][k] + terms[2][k] for k in range(2)]
        even_diff = [terms[0][k] - terms[2][k] for k in range(2)]
        odd_sum = [terms[1][k] + terms[3][k] for k in range(2)]
        odd_diff = [terms[3][1] - terms[1][1], terms[1][0] - terms[3][0]]
        results = (
            [even_sum[k] + odd_sum[k] for k in range(2)],
            [even_diff[k] + odd_diff[k] for k in range(2)],
            [even_sum[k] - odd_sum[k] for k in range(2)],
            [even_diff[k] - odd_diff[k] for k in range(2)],
        )
        for block, result in enumerate(results):
            for k in range(2):
                lines[pl.ds(block * share, share), :, :, :, pl.ds(k * FP + start, width)] = (
                    result[k].astype(BF16).reshape(share, 2, 2, rows, width)
                )
    pl.semaphore_wait(barrier, length + 1)

    copies = []
    for step in order:
        target = lax.rem(place + step, length)
        copy = pltpu.make_async_remote_copy(
            src_ref=lines.at[target, :, 1 - core],
            dst_ref=pair.at[target],
            send_sem=pair_send.at[step],
            recv_sem=pair_recv.at[step],
            device_id=device(place, side, 1 - core),
            device_id_type=MESH,
        )
        copy.start()
        copies.append(copy)
    beside_copies = []
    for step, copy in zip(order, copies):
        target = lax.rem(place + step, length)
        copy.wait_recv()
        beside_out[target] = (
            lines[target, 1 - side, core].astype(F32) + pair[target, 1 - side].astype(F32)
        ).astype(BF16)
        onward = pltpu.make_async_remote_copy(
            src_ref=beside_out.at[target],
            dst_ref=beside.at[target],
            send_sem=beside_send.at[step],
            recv_sem=beside_recv.at[step],
            device_id=device(place, 1 - side, core),
            device_id_type=MESH,
        )
        onward.start()
        beside_copies.append(onward)
    ring_copies = []
    for step, copy in zip(order, beside_copies):
        target = lax.rem(place + step, length)
        copy.wait_recv()
        value = (
            lines[target, side, core].astype(F32)
            + pair[target, side].astype(F32)
            + beside[target].astype(F32)
        )
        if step == 0:
            total = value
            continue
        ring_out[target] = value.astype(BF16)
        onward = pltpu.make_async_remote_copy(
            src_ref=ring_out.at[target],
            dst_ref=ring.at[place],
            send_sem=ring_send.at[step],
            recv_sem=ring_recv.at[step],
            device_id=device(target, side, core),
            device_id_type=MESH,
        )
        onward.start()
        ring_copies.append(onward)
    for step, copy in zip(order, ring_copies):
        copy.wait_recv()
        total = total + ring[lax.rem(place + length - step, length)].astype(F32)
    total = total.astype(BF16)
    real, imag = total[:, :FP], total[:, FP:]
    cos_part, sin_part = edge_ref[:, :FP], edge_ref[:, FP:]
    out_ref[0] = (dot(real, cos_part) - dot(imag, sin_part)) * scale
    out_ref[1] = (dot(real, sin_part) + dot(imag, cos_part)) * scale
    for copy in copies + beside_copies + ring_copies:
        copy.wait_send()


def sum_facet(folded, scale, times):
    length = times // 4
    rows = FP // times
    vmem = pl.BlockSpec(memory_space=pltpu.VMEM)
    block = pltpu.VMEM((length, rows, 2 * FP), BF16)
    return pl.pallas_call(
        functools.partial(sum_kernel, scale, times),
        out_shape=jax.ShapeDtypeStruct((2, rows, FP), F32),
        in_specs=[vmem] * 3,
        out_specs=vmem,
        scratch_shapes=[
            pltpu.VMEM((length, 2, 2, rows, 2 * FP), BF16),
            pltpu.VMEM((length, 2, rows, 2 * FP), BF16),
            block,
            block,
            block,
            block,
        ]
        + [pltpu.SemaphoreType.DMA((length,))] * 6,
        compiler_params=pltpu.CompilerParams(
            collective_id=1, has_side_effects=True, vmem_limit_bytes=VMEM_LIMIT
        ),
        name="sum_facet",
    )(folded, jnp.asarray(facet_rows_table()), jnp.asarray(facet_table()))


def per_device(
    visibilities, coordinates, station_screens, subgrid_stations, subgrid_corners, facet_member
):
    times = lax.axis_size("tm")
    facets = lax.axis_size("facet")
    facet = lax.axis_index("facet")
    screens = jnp.transpose(
        lax.dynamic_slice_in_dim(station_screens, facet * LANES, LANES, axis=3), (0, 2, 1, 3)
    )
    mixed = gather_rows(
        visibilities, coordinates, screens, jnp.transpose(subgrid_stations), facets, times
    )
    folded = fold_facet(facet, jnp.transpose(subgrid_corners), jnp.transpose(facet_member), mixed)
    total_count = visibilities.shape[1] * facets * times
    scale = 1.0 / (S * math.sqrt(visibilities.shape[2] * total_count))
    own_rows = sum_facet(folded, scale, times)
    return own_rows[:, None]


def solution(mesh):
    in_specs = (
        P(None, ("tm", "facet"), None),
        P(None, ("tm", "facet"), None),
        P(None, "tm", None, None),
        P("tm", None),
        P("tm", None),
        P("tm", "facet"),
    )
    out_specs = P(None, "facet", "tm", None)
    return jax.shard_map(
        per_device, mesh=mesh, in_specs=in_specs, out_specs=out_specs, check_vma=False
    )
```
